32 devices in a mesh: grp: 2 (over y), mon: 4 (over z), pair: 2 (over x), sub: 2 (over core).
Axes of the slice: x: 2, y: 2, z: 4, core: 2. Of those that a mesh axis runs over, the one named last changes fastest.
Arguments:
- dfactors: bfloat16 [8192, 1024], P('mon', 'sub'), may hold values from -0.5 to 0.5
- block_mask: int32 [64, 1024], P('mon', 'sub'), may hold values 0 or 1
- base_flow: float32 [8192], P('mon'), may hold values from -5 to 5
- branch_row: int32 [1024], replicated, may hold values from 0 to 8191, as said below
- pair_slots: int32 [3072, 2], P(('grp', 'pair')), parts along dimension 0, may hold values from 0 to 1023, as said below
- pair_counts: int32 [4], P(('grp', 'pair')), parts along dimension 0, may hold values from 1 to 768, 1024 in all
Outputs:
- post_flows: bfloat16 [8192, 3072], P(('mon', 'sub'), ('grp', 'pair')), parts along dimension 1
The draws below stay inside these ranges and needn't reach their ends.
There are 2 independent parts, one for each index of `grp`. The reference program is written for one: setup_inputs(seed, part) draws one part's arguments, and reference() takes and returns one part's arrays. A program takes and returns all parts, laid end to end along the dimension named above; an argument that names none is the same for every part. Nothing has to cross between parts.
Inputs may be any that keep to these rules, and one draw needn't show every extreme that they name: `branch_row`: all entries distinct. `pair_slots`: the two candidates of a slot differ; empty slots hold valid pairs too. `pair_counts`: the counts sum to 1024; an owner's live slots are its first ones.
All inputs are finite; a program needn't handle non-finite values. No bound on the sum of `block_mask` or of `pair_counts` on one device may be relied on, other than what follows from the above.
Results may differ from the reference program's by a relative error of at most 0.004.
Values may be sent and summed in bfloat16 or wider, within the bound.
A program may use at most 64 MiB of HBM per device.

```python
import math
import jax
import jax.numpy as jnp
import numpy as np
from jax import lax

BLOCK = 128
C = 1024
MB_DEV = 16
M = 8192
PAIRS = 1024
PCAP = 768
SLOTS = 1536
N_MON = 4
N_PAIR = 2
N_SUB = 2


def draw_branch_row(key, part):
    return jax.random.permutation(jax.random.fold_in(key, 11), M)[:C].astype(jnp.int32)


def draw_pair_slots(key, part):
    first_out = jax.random.randint(jax.random.fold_in(key, 21), (SLOTS,), 0, C)
    offset_draw = jax.random.randint(jax.random.fold_in(key, 22), (SLOTS,), 1, C)
    second_out = (first_out + offset_draw) % C
    first_out = first_out.at[0].set(C - 1)
    second_out = second_out.at[0].set(0)
    return jnp.stack([first_out, second_out], axis=1).astype(jnp.int32)


def place_ends(drawn, stream_key, least, high):
    spot = [jax.random.randint(jax.random.fold_in(stream_key, axis), (), 0, length) for axis, length in enumerate(drawn.shape)]
    widest = drawn.shape.index(max(drawn.shape))
    next_to = spot[:widest] + [(spot[widest] + 1) % drawn.shape[widest]] + spot[widest + 1:]
    return drawn.at[tuple(spot)].set(least).at[tuple(next_to)].set(high)


def shard_levels(own_key, extent, shards, smallest, top_value):
    def one(dim, blocks):
        heights = jax.random.uniform(jax.random.fold_in(jax.random.fold_in(own_key, 6), dim), (blocks,), jnp.float32, smallest / len(shards), top_value / len(shards))
        return jnp.repeat(jnp.exp(heights), extent[dim] // blocks).reshape((-1,) + (1,) * (len(extent) - dim - 1))

    gain = one(*shards[0])
    for cut in shards[1:]:
        gain = gain * one(*cut)
    return gain


def length_profile(amount, total, most, skew):
    weights = [(1 << 20) // math.isqrt(grade ** skew) + 1 for grade in range(2, amount + 1)]
    spare, given = total - most - (amount - 1), [1] * (amount - 1)
    while spare > 0:
        free = [i for i in range(amount - 1) if given[i] < most]
        whole, left = sum([weights[i] for i in free]), spare
        for i in free:
            more = min(most - given[i], max(1, left * weights[i] // whole), spare)
            given[i] = given[i] + more
            spare = spare - more
    return np.array([most] + given)


def ragged_sizes(key, amount, total, reach, slope):
    if amount == 2:
        one = jax.random.randint(key, (), max(1, total - reach), min(reach, total - 1) + 1)
        return jnp.stack([one, total - one])
    sizes = jnp.asarray(length_profile(amount, total, reach, slope), jnp.int32)
    twos = (amount - 1) // 2
    donor, sink = sizes[1:1 + 2 * twos:2], sizes[2:2 + 2 * twos:2]
    slack = jnp.minimum(donor - 1, reach - sink)
    shifted = jax.random.randint(jax.random.fold_in(key, 1), (twos,), 0, 1 << 20) % (slack + 1)
    sizes = sizes.at[1:1 + 2 * twos:2].set(donor - shifted).at[2:2 + 2 * twos:2].set(sink + shifted)
    return sizes[jax.random.permutation(jax.random.fold_in(key, 2), amount)]


def scatter_about(stream_key, extent, deviation, most, split=(), kind=jnp.bfloat16):
    drawn = jax.random.normal(stream_key, extent, jnp.float32) * deviation
    if len(split) > 0:
        drawn = shard_levels(stream_key, extent, split, -0.22, 0.18) * drawn
    return jnp.clip(drawn, min=-most, max=most).astype(kind)


def setup_inputs(seed: int = 0, part: int = 0) -> dict:
    keys = jax.random.split(jax.random.key(seed), 7)
    own_keys = jax.random.split(jax.random.fold_in(keys[6], part), 7)
    dfactors = jnp.clip(jax.random.uniform(keys[0], (M, C), jnp.float32, -0.5, 0.5) * shard_levels(keys[0], (M, C), ((0, 4), (1, 2)), -0.4, 0.0), -0.5, 0.5).astype(jnp.bfloat16)
    block_mask = place_ends((jax.random.randint(keys[1], (M // BLOCK, C), 0, 4) < 3).astype(jnp.int32), jax.random.fold_in(keys[1], 1), 0, 1)
    base_flow = scatter_about(keys[2], (M,), 1.0, 5.0, ((0, 4),), jnp.float32)
    branch_row = draw_branch_row(jax.random.fold_in(keys[6], 71), part)
    pair_slots = draw_pair_slots(jax.random.fold_in(jax.random.fold_in(keys[6], part), 71), part)
    pair_counts = ragged_sizes(own_keys[5], N_PAIR, PAIRS, PCAP, 2).astype(jnp.int32)
    return {"dfactors": dfactors, "block_mask": block_mask, "base_flow": base_flow, "branch_row": branch_row, "pair_slots": pair_slots, "pair_counts": pair_counts}


def reference(dfactors, block_mask, base_flow, branch_row, pair_slots, pair_counts):
    col_width = C // N_SUB
    block_keep = jnp.repeat(block_mask.astype(jnp.bfloat16), BLOCK, axis=0)
    masked = dfactors * block_keep
    first_out = pair_slots[:, 0]
    second_out = pair_slots[:, 1]
    first_row = branch_row[first_out]
    second_row = branch_row[second_out]
    cross_first = masked[first_row, second_out].astype(jnp.float32)
    cross_second = masked[second_row, first_out].astype(jnp.float32)
    flow_first = base_flow[first_row]
    flow_second = base_flow[second_row]
    determinant = 1.0 - cross_first * cross_second
    shift_first = (flow_first + cross_first * flow_second) / determinant
    shift_second = (flow_second + cross_second * flow_first) / determinant
    columns = jnp.arange(C, dtype=jnp.int32)[:, None]
    shift = (jnp.where(columns == first_out[None, :], shift_first[None, :], jnp.float32(0.0))
             + jnp.where(columns == second_out[None, :], shift_second[None, :], jnp.float32(0.0))).astype(jnp.bfloat16)
    slot_ids = jnp.arange(SLOTS, dtype=jnp.int32)
    live_slot = ((slot_ids % PCAP) < pair_counts[slot_ids // PCAP]).astype(jnp.float32)
    row_blocks = masked.reshape(N_MON, MB_DEV * BLOCK, C)
    flow_blocks = base_flow.reshape(N_MON, MB_DEV * BLOCK)

    def one_block(inputs):
        rows_here, flows_here = inputs
        total = jnp.zeros((rows_here.shape[0], SLOTS), jnp.float32)
        for which in range(N_SUB):
            partial_value = jnp.dot(rows_here[:, which * col_width:(which + 1) * col_width],
                              shift[which * col_width:(which + 1) * col_width],
                              preferred_element_type=jnp.float32).astype(jnp.bfloat16)
            total = total + lax.optimization_barrier(partial_value).astype(jnp.float32)
        return ((flows_here[:, None] + total) * live_slot[None, :]).astype(jnp.bfloat16)

    result = lax.map(one_block, (row_blocks, flow_blocks))
    return result.reshape(M, SLOTS)
```

```python
import functools

import jax
import jax.numpy as jnp
from jax import lax
from jax.experimental import pallas as pl
from jax.experimental.pallas import tpu as pltpu
from jax.sharding import PartitionSpec as P

BLOCK = 128
LOT = 256
MESH = pl.DeviceIdType.MESH
F32 = jnp.float32
BF16 = jnp.bfloat16
I32 = jnp.int32


def lookup(table, index):
    groups = []
    height = table.shape[0]
    for start in range(0, index.shape[1], 128):
        wide = jnp.broadcast_to(index[:, start:start + 128], (height, 128))
        lanes = jnp.take_along_axis(table, wide & 127, axis=1)
        level = lax.broadcasted_iota(I32, (height, 128), 0)
        picked = jnp.where(level == (wide >> 7), lanes, jnp.zeros_like(lanes))
        groups.append(jnp.sum(picked, axis=0, keepdims=True))
    return jnp.concatenate(groups, axis=1)


def ones_where(condition):
    return jnp.where(condition, F32(1), F32(0)).astype(BF16)


def spread_lot(place_ref, lot, groups, spread_ref):
    level = lax.broadcasted_iota(I32, (LOT, BLOCK), 0) + lot * LOT
    for g in range(groups):
        spread_ref[:, g * BLOCK:(g + 1) * BLOCK] = ones_where(level == place_ref[g:g + 1, :])


def wanted_of(values, spread):
    picked = lax.dot_general(values, spread, (((1,), (1,)), ((), ())), preferred_element_type=F32).astype(I32)
    filled = picked[4:5] > 0
    row = jnp.where(filled, picked[0:1] * 256 + picked[1:2], -1)
    column = jnp.where(filled, picked[2:3] * 256 + picked[3:4], -1)
    return row, column


def found_of(parts, mask, hot, row):
    found = jnp.zeros((1, LOT), F32)
    start = 0
    for part in parts:
        near = jnp.dot(part, hot, preferred_element_type=F32)
        level = lax.broadcasted_iota(I32, near.shape, 0) + start
        found = found + jnp.sum(jnp.where(level == row, near, F32(0)), axis=0, keepdims=True)
        start += part.shape[0]
    kept = jnp.dot(mask, hot, preferred_element_type=F32)
    level = lax.broadcasted_iota(I32, kept.shape, 0)
    return found * jnp.sum(jnp.where(level == (row >> 7), kept, F32(0)), axis=0, keepdims=True)


def scatter(found, spread):
    wide = jnp.broadcast_to(found, (8, LOT)).astype(BF16)
    return jnp.dot(wide, spread, preferred_element_type=F32)[0:1]


def head_kernel(n_sub, df_hbm, mask_hbm, base_hbm, row_hbm, pair_hbm, count_s,
                both, rest, mask, pair_v, base_v, flow, values, place, hot, wanted, spread, total_s,
                row_v, mask_v, far_mask, load_sem, part_send, part_recv):
    rows_dev, width = df_hbm.shape
    half = rows_dev // n_sub
    blocks = half // BLOCK
    capacity = pair_hbm.shape[1]
    groups = 2 * capacity // BLOCK
    mon = lax.axis_index("mon")
    sub = lax.axis_index("sub")
    other = 1 - sub
    partner = {"sub": other}

    barrier = pltpu.get_barrier_semaphore()
    pl.semaphore_signal(barrier, inc=1, device_id=partner, device_id_type=MESH)
    near_columns = pl.ds(0, width)
    loads = [
        pltpu.make_async_copy(row_hbm, row_v, load_sem.at[0]),
        pltpu.make_async_copy(pair_hbm, pair_v, load_sem.at[1]),
        pltpu.make_async_copy(df_hbm.at[pl.ds(sub * half, half)], both.at[pl.ds(0, half), near_columns], load_sem.at[2]),
        pltpu.make_async_copy(df_hbm.at[pl.ds(other * half, half)], rest, load_sem.at[3]),
        pltpu.make_async_copy(mask_hbm, mask_v, load_sem.at[4]),
        pltpu.make_async_copy(base_hbm.at[pl.ds(sub * blocks, blocks)], base_v, load_sem.at[5]),
    ]
    for load in loads:
        load.start()
    part_copies = [
        pltpu.make_async_remote_copy(
            df_hbm.at[pl.ds(other * half, half)], both.at[pl.ds(0, half), pl.ds(width, width)],
            part_send.at[0], part_recv.at[0], device_id=partner, device_id_type=MESH),
        pltpu.make_async_remote_copy(
            mask_hbm.at[pl.ds(other * blocks, blocks)], far_mask,
            part_send.at[1], part_recv.at[1], device_id=partner, device_id_type=MESH),
    ]
    pl.semaphore_wait(barrier, 1)
    for copy in part_copies:
        copy.start()

    loads[0].wait()
    loads[1].wait()
    table = row_v[...]
    first, second = pair_v[0:1, :], pair_v[1:2, :]
    first_row, second_row = lookup(table, first), lookup(table, second)
    row = jnp.concatenate([first_row, second_row], axis=1) - mon * rows_dev
    column = jnp.concatenate([second, first], axis=1) - sub * width
    slot = lax.broadcasted_iota(I32, (1, capacity), 1)
    live = slot < count_s[0]
    live = jnp.concatenate([live, live], axis=1)
    local = (row >= 0) & (row < rows_dev) & (column >= 0) & (column < width) & live
    flags = jnp.where(local, F32(1), F32(0))
    running = jnp.zeros((1, BLOCK), F32)
    flag_rows, before_rows = [], []
    for g in range(groups):
        flag_rows.append(flags[:, g * BLOCK:(g + 1) * BLOCK])
        before_rows.append(running)
        running = running + flag_rows[-1]
    padding = [jnp.zeros((1, BLOCK), F32)] * (place.shape[0] - groups)
    flag_grid = jnp.concatenate(flag_rows + padding, axis=0)
    counted = jnp.concatenate([flag_grid, jnp.concatenate(before_rows + padding, axis=0)], axis=1)
    across = lax.broadcasted_iota(I32, (2 * BLOCK, BLOCK), 0)
    down = lax.broadcasted_iota(I32, (2 * BLOCK, BLOCK), 1)
    adder = ones_where((across < down) | (across >= BLOCK))
    order = jnp.dot(counted.astype(BF16), adder, preferred_element_type=F32).astype(I32)
    place[...] = jnp.where(flag_grid > 0, order, -1)
    zero = jnp.zeros_like(row)
    stacked = jnp.concatenate([row >> 8, row & 255, column >> 8, column & 255, zero + 1, zero, zero, zero], axis=0)
    values[...] = stacked.astype(F32).astype(BF16)
    spread_lot(place, 0, groups, spread)
    wanted_row, wanted_column = wanted_of(values[...], spread[...])
    wanted[...] = wanted_row
    level = lax.broadcasted_iota(I32, (width, LOT), 0)
    hot[...] = ones_where(level == wanted_column)
    total_s[0] = jnp.sum(running).astype(I32)

    loads[5].wait()
    base = base_v[...]
    flow_start = mon * rows_dev + sub * half
    flow[0:1, :] = lookup(base, first_row - flow_start)
    flow[1:2, :] = lookup(base, second_row - flow_start)
    loads[4].wait()
    whole = mask_v[...].astype(F32)
    own, off = whole[:blocks], whole[blocks:]
    swapped = sub != 0
    mine, theirs = jnp.where(swapped, off, own), jnp.where(swapped, own, off)
    mask[...] = jnp.concatenate([mine, theirs], axis=0).astype(BF16)
    for load in loads[2:4]:
        load.wait()
    for copy in part_copies:
        copy.wait_recv()
    far = far_mask[...].astype(F32)
    pad = jnp.zeros((both.shape[0] - half - blocks, 2 * width), F32)
    both[half:, :] = jnp.concatenate([jnp.concatenate([mine, far], axis=1), pad], axis=0).astype(BF16)
    for copy in part_copies:
        copy.wait_send()


def order_rows(row, half, sub):
    flipped = jnp.where(row >= half, row - half, row + half)
    return jnp.where(row < 0, -1, jnp.where(sub == 0, row, flipped))


def spare_kernel(both, rest, mask, values, place, total_s, extra, spread):
    half, width = rest.shape
    capacity = extra.shape[1]
    groups = 2 * capacity // BLOCK
    sub = lax.axis_index("sub")
    extra[...] = jnp.zeros_like(extra)

    def one_lot(lot, carry):
        spread_lot(place, lot, groups, spread)
        row, column = wanted_of(values[...], spread[...])
        row = order_rows(row, half, sub)
        level = lax.broadcasted_iota(I32, (width, LOT), 0)
        hot = ones_where(level == column)
        found = found_of([both[0:half, 0:width], rest[...]], mask[...], hot, row)
        cross = scatter(found, spread[...])
        extra[0:1, :] += cross[:, :capacity]
        extra[1:2, :] += cross[:, capacity:]
        return carry

    lax.fori_loop(1, (total_s[0] + LOT - 1) // LOT, one_lot, 0)


def main_kernel(n_mon, n_sub, chunk, both, rest, mask, pair_v, base_v, flow, hot, wanted, spread, extra, count_s,
                product, keep, shifts, base_wide,
                told, got, send_sem, recv_sem):
    half, width = rest.shape
    blocks = half // BLOCK
    capacity = pair_v.shape[1]
    chunks = capacity // chunk
    n = n_mon * n_sub
    mon = lax.axis_index("mon")
    sub = lax.axis_index("sub")
    me = mon * n_sub + sub

    def peer(step):
        flat = lax.rem(me + step, n)
        return {"mon": flat // n_sub, "sub": lax.rem(flat, n_sub)}

    barrier = pltpu.get_barrier_semaphore()

    def greet(step, carry):
        pl.semaphore_signal(barrier, inc=1, device_id=peer(step), device_id_type=MESH)
        return carry

    lax.fori_loop(1, n, greet, 0)
    row = order_rows(wanted[...], half, sub)
    found = found_of([both[0:half, 0:width], rest[...]], mask[...], hot[...], row)
    cross = scatter(found, spread[...])
    told[0:1, :] = cross[:, :capacity] + extra[0:1, :]
    told[1:2, :] = cross[:, capacity:] + extra[1:2, :]
    told[2:4, :] = flow[...]

    def products():
        def one_chunk(c, carry):
            span = pl.ds(pl.multiple_of(c * chunk, chunk), chunk)
            columns = jnp.concatenate([pair_v[0:1, span], pair_v[1:2, span]], axis=1) - sub * width
            columns = jnp.where(columns < 0, columns + n_sub * width, columns)
            level = lax.broadcasted_iota(I32, (n_sub * width, 2 * chunk), 0)
            made = jnp.dot(both[...], ones_where(level == columns), preferred_element_type=F32)
            product[c] = made[:half]
            keep[c] = made[half:half + blocks]
            return carry

        lax.fori_loop(0, chunks, one_chunk, 0)

    @pl.when(mon == 0)
    def _():
        products()

    pl.semaphore_wait(barrier, n - 1)

    def send(step, carry):
        pltpu.make_async_remote_copy(
            told, got.at[step - 1], send_sem, recv_sem, device_id=peer(step), device_id_type=MESH).start()
        return carry

    lax.fori_loop(1, n, send, 0)
    base = base_v[...]
    for b in range(blocks):
        base_wide[b * BLOCK:(b + 1) * BLOCK, :] = jnp.broadcast_to(base[b:b + 1, :], (BLOCK, BLOCK)).T

    @pl.when(mon != 0)
    def _():
        products()

    live = (lax.broadcasted_iota(I32, (1, capacity), 1) < count_s[0]).astype(F32)
    pltpu.make_async_copy(got, got, recv_sem).wait()
    heard = told[...] + jnp.sum(got[...], axis=0)
    cross_first, cross_second, flow_first, flow_second = [heard[i:i + 1] for i in range(4)]
    determinant = 1.0 - cross_first * cross_second
    shift_first = (flow_first + cross_first * flow_second) / determinant
    shift_second = (flow_second + cross_second * flow_first) / determinant
    shifts[0:1, :] = shift_first.astype(BF16).astype(F32) * live
    shifts[1:2, :] = shift_second.astype(BF16).astype(F32) * live
    shifts[2:3, :] = live
    pltpu.make_async_copy(got, got, send_sem).wait()


def last_kernel(product, keep, shifts, base_wide, out_hbm, out_v, sems):
    chunks, half, pair_width = product.shape
    chunk = pair_width // 2
    copies = []
    for b in range(half // BLOCK):
        rows = slice(b * BLOCK, (b + 1) * BLOCK)
        flows = jnp.concatenate([base_wide[rows, :]] * (chunk // BLOCK), axis=1)
        for c in range(chunks):
            span = slice(c * chunk, (c + 1) * chunk)
            effect_first = shifts[0:1, span] * keep[c, b:b + 1, :chunk]
            effect_second = shifts[1:2, span] * keep[c, b:b + 1, chunk:]
            value = flows * shifts[2:3, span] + product[c, rows, :chunk] * effect_first
            value = value + product[c, rows, chunk:] * effect_second
            out_v[rows, span] = value.astype(BF16)
        place = pl.ds(b * BLOCK, BLOCK)
        copies.append(pltpu.make_async_copy(out_v.at[place], out_hbm.at[place], sems.at[b]))
        copies[-1].start()
    for copy in copies:
        copy.wait()


def on_device(n_mon, n_sub, dfactors, block_mask, base_flow, branch_row, pair_slots, pair_counts):
    rows_dev, width = dfactors.shape
    half = rows_dev // n_sub
    blocks = half // BLOCK
    capacity = pair_slots.shape[0]
    chunk = 256 if capacity % 256 == 0 else BLOCK
    chunks = capacity // chunk
    groups = 2 * capacity // BLOCK
    padded = -(-groups // 8) * 8
    n = n_mon * n_sub
    any_spec = pl.BlockSpec(memory_space=pltpu.HBM)
    vmem_spec = pl.BlockSpec(memory_space=pltpu.VMEM)
    smem_spec = pl.BlockSpec(memory_space=pltpu.SMEM)
    dma = pltpu.SemaphoreType.DMA

    def params(mib, **more):
        return pltpu.CompilerParams(vmem_limit_bytes=int(mib * 1024 * 1024), **more)

    def kept(arrays):
        return [pltpu.with_memory_space_constraint(array, pltpu.VMEM) for array in arrays]

    *made, total = pl.pallas_call(
        functools.partial(head_kernel, n_sub),
        out_shape=[
            pltpu.VMEM((half + 16, n_sub * width), BF16),
            pltpu.VMEM((half, width), BF16),
            pltpu.VMEM((n_sub * blocks, width), BF16),
            pltpu.VMEM((2, capacity), I32),
            pltpu.VMEM((blocks, BLOCK), F32),
            pltpu.VMEM((2, capacity), F32),
            pltpu.VMEM((8, 2 * capacity), BF16),
            pltpu.VMEM((padded, BLOCK), I32),
            pltpu.VMEM((width, LOT), BF16),
            pltpu.VMEM((1, LOT), I32),
            pltpu.VMEM((LOT, 2 * capacity), BF16),
            pltpu.SMEM((1,), I32),
        ],
        in_specs=[any_spec] * 5 + [smem_spec],
        out_specs=[vmem_spec] * 11 + [smem_spec],
        scratch_shapes=[
            pltpu.VMEM((branch_row.shape[0] // BLOCK, BLOCK), I32),
            pltpu.VMEM((n_sub * blocks, width), I32),
            pltpu.VMEM((blocks, width), I32),
            dma((6,)), dma((2,)), dma((2,)),
        ],
        compiler_params=params(58.8, collective_id=0, has_side_effects=True),
    )(dfactors, block_mask, base_flow.reshape(-1, BLOCK), branch_row.reshape(-1, BLOCK), pair_slots.T, pair_counts)
    both, rest, mask, pair_v, base_v, flow, values, place, hot, wanted, spread = kept(made)
    extra = pl.pallas_call(
        spare_kernel,
        out_shape=pltpu.VMEM((2, capacity), F32),
        in_specs=[vmem_spec] * 5 + [smem_spec],
        out_specs=vmem_spec,
        scratch_shapes=[pltpu.VMEM((LOT, 2 * capacity), BF16)],
        compiler_params=params(24),
    )(both, rest, mask, values, place, total)
    made = pl.pallas_call(
        functools.partial(main_kernel, n_mon, n_sub, chunk),
        out_shape=[
            pltpu.VMEM((chunks, half, 2 * chunk), F32),
            pltpu.VMEM((chunks, blocks, 2 * chunk), F32),
            pltpu.VMEM((3, capacity), F32),
            pltpu.VMEM((half, BLOCK), F32),
        ],
        in_specs=[vmem_spec] * 10 + [smem_spec],
        out_specs=[vmem_spec] * 4,
        scratch_shapes=[
            pltpu.VMEM((4, capacity), F32),
            pltpu.VMEM((n - 1, 4, capacity), F32),
            dma, dma,
        ],
        compiler_params=params(40, collective_id=1, has_side_effects=True),
    )(both, rest, mask, pair_v, base_v, flow, hot, wanted, spread, kept([extra])[0], pair_counts)
    return pl.pallas_call(
        last_kernel,
        out_shape=jax.ShapeDtypeStruct((half, capacity), BF16),
        in_specs=[vmem_spec] * 4,
        out_specs=any_spec,
        scratch_shapes=[pltpu.VMEM((half, capacity), BF16), dma((blocks,))],
        compiler_params=params(16),
    )(*kept(made))


def solution(mesh):
    return jax.shard_map(
        functools.partial(on_device, mesh.shape["mon"], mesh.shape["sub"]),
        mesh=mesh,
        in_specs=(
            P("mon", "sub"),
            P("mon", "sub"),
            P("mon"),
            P(),
            P(("grp", "pair"), None),
            P(("grp", "pair")),
        ),
        out_specs=P(("mon", "sub"), ("grp", "pair")),
        check_vma=False,
    )
```

```python
import functools

import jax
import jax.numpy as jnp
from jax import lax
from jax.experimental import pallas as pl
from jax.experimental.pallas import tpu as pltpu
from jax.sharding import PartitionSpec as P

BLOCK = 128
LOT = 256
MESH = pl.DeviceIdType.MESH
F32 = jnp.float32
BF16 = jnp.bfloat16
I32 = jnp.int32


def lookup(table, index):
    groups = []
    height = table.shape[0]
    for start in range(0, index.shape[1], 128):
        wide = jnp.broadcast_to(index[:, start:start + 128], (height, 128))
        lanes = jnp.take_along_axis(table, wide & 127, axis=1)
        level = lax.broadcasted_iota(I32, (height, 128), 0)
        picked = jnp.where(level == (wide >> 7), lanes, jnp.zeros_like(lanes))
        groups.append(jnp.sum(picked, axis=0, keepdims=True))
    return jnp.concatenate(groups, axis=1)


def stack_groups(wide, height):
    rows = [wide[:, start:start + BLOCK] for start in range(0, wide.shape[1], BLOCK)]
    rows += [jnp.zeros((1, BLOCK), wide.dtype)] * (height - len(rows))
    return jnp.concatenate(rows, axis=0)


def ones_where(condition):
    return jnp.where(condition, F32(1), F32(0)).astype(BF16)


def spread_lot(place_ref, lot, groups, spread_ref):
    level = lax.broadcasted_iota(I32, (LOT, BLOCK), 0) + lot * LOT
    for g in range(groups):
        spread_ref[:, g * BLOCK:(g + 1) * BLOCK] = ones_where(level == place_ref[g:g + 1, :])


def wanted_of(values, spread):
    picked = lax.dot_general(values, spread, (((1,), (1,)), ((), ())), preferred_element_type=F32).astype(I32)
    filled = picked[4:5] > 0
    row = jnp.where(filled, picked[0:1] * 256 + picked[1:2], -1)
    column = jnp.where(filled, picked[2:3] * 256 + picked[3:4], -1)
    return row, column


def found_of(parts, mask, hot, row):
    found = jnp.zeros((1, LOT), F32)
    start = 0
    for part in parts:
        near = jnp.dot(part, hot, preferred_element_type=F32)
        level = lax.broadcasted_iota(I32, near.shape, 0) + start
        found = found + jnp.sum(jnp.where(level == row, near, F32(0)), axis=0, keepdims=True)
        start += part.shape[0]
    kept = jnp.dot(mask, hot, preferred_element_type=F32)
    level = lax.broadcasted_iota(I32, kept.shape, 0)
    return found * jnp.sum(jnp.where(level == (row >> 7), kept, F32(0)), axis=0, keepdims=True)


def scatter(found, spread):
    wide = jnp.broadcast_to(found, (8, LOT)).astype(BF16)
    return jnp.dot(wide, spread, preferred_element_type=F32)[0:1]


def padded_rows(rows):
    pad = jnp.zeros((-rows.shape[0] % 16, rows.shape[1]), F32)
    return jnp.concatenate([rows, pad], axis=0).astype(BF16)


def head_kernel(n_sub, df_hbm, mask_hbm, base_hbm, row_hbm, pair_hbm, count_s,
                own, far, rest, mask, pair_v, base_v, flow, values, place, hot, wanted, spread, total_s,
                row_v, mask_v, far_mask, load_sem, part_send, part_recv):
    rows_dev, width = df_hbm.shape
    half = rows_dev // n_sub
    blocks = half // BLOCK
    capacity = pair_hbm.shape[1]
    groups = 2 * capacity // BLOCK
    mon = lax.axis_index("mon")
    sub = lax.axis_index("sub")
    other = 1 - sub
    partner = {"sub": other}

    barrier = pltpu.get_barrier_semaphore()

    @pl.when(mon == 0)
    def _():
        pl.semaphore_signal(barrier, inc=1, device_id=partner, device_id_type=MESH)

    loads = [
        pltpu.make_async_copy(row_hbm, row_v, load_sem.at[0]),
        pltpu.make_async_copy(pair_hbm, pair_v, load_sem.at[1]),
        pltpu.make_async_copy(df_hbm.at[pl.ds(sub * half, half)], own.at[pl.ds(0, half)], load_sem.at[2]),
        pltpu.make_async_copy(df_hbm.at[pl.ds(other * half, half)], rest, load_sem.at[3]),
        pltpu.make_async_copy(mask_hbm, mask_v, load_sem.at[4]),
        pltpu.make_async_copy(base_hbm, base_v, load_sem.at[5]),
    ]
    for load in loads:
        load.start()
    part_copies = [
        pltpu.make_async_remote_copy(
            df_hbm.at[pl.ds(other * half, half)], far.at[pl.ds(0, half)],
            part_send.at[0], part_recv.at[0], device_id=partner, device_id_type=MESH),
        pltpu.make_async_remote_copy(
            mask_hbm.at[pl.ds(other * blocks, blocks)], far_mask,
            part_send.at[1], part_recv.at[1], device_id=partner, device_id_type=MESH),
    ]

    @pl.when(mon == 0)
    def _():
        pl.semaphore_wait(barrier, 1)
        for copy in part_copies:
            copy.start()

    loads[0].wait()
    loads[1].wait()
    table = row_v[...]
    first, second = pair_v[0:1, :], pair_v[1:2, :]
    first_row, second_row = lookup(table, first), lookup(table, second)
    row = jnp.concatenate([first_row, second_row], axis=1) - mon * rows_dev
    column = jnp.concatenate([second, first], axis=1) - sub * width
    slot = lax.broadcasted_iota(I32, (1, capacity), 1)
    live = slot < count_s[0]
    live = jnp.concatenate([live, live], axis=1)
    local = (row >= 0) & (row < rows_dev) & (column >= 0) & (column < width) & live
    flags = jnp.where(local, F32(1), F32(0))
    running = jnp.zeros((1, BLOCK), F32)
    flag_rows, before_rows = [], []
    for g in range(groups):
        flag_rows.append(flags[:, g * BLOCK:(g + 1) * BLOCK])
        before_rows.append(running)
        running = running + flag_rows[-1]
    padding = [jnp.zeros((1, BLOCK), F32)] * (place.shape[0] - groups)
    flag_grid = jnp.concatenate(flag_rows + padding, axis=0)
    counted = jnp.concatenate([flag_grid, jnp.concatenate(before_rows + padding, axis=0)], axis=1)
    across = lax.broadcasted_iota(I32, (2 * BLOCK, BLOCK), 0)
    down = lax.broadcasted_iota(I32, (2 * BLOCK, BLOCK), 1)
    adder = ones_where((across < down) | (across >= BLOCK))
    order = jnp.dot(counted.astype(BF16), adder, preferred_element_type=F32).astype(I32)
    place[...] = jnp.where(flag_grid > 0, order, -1)
    zero = jnp.zeros_like(row)
    stacked = jnp.concatenate([row >> 8, row & 255, column >> 8, column & 255, zero + 1, zero, zero, zero], axis=0)
    values[...] = stacked.astype(F32).astype(BF16)
    spread_lot(place, 0, groups, spread)
    wanted_row, wanted_column = wanted_of(values[...], spread[...])
    wanted[...] = wanted_row
    level = lax.broadcasted_iota(I32, (width, LOT), 0)
    hot[...] = ones_where(level == wanted_column)
    total_s[0] = jnp.sum(running).astype(I32)

    loads[5].wait()
    base = base_v[...]
    flow[...] = stack_groups(lookup(base, row), flow.shape[0])
    loads[4].wait()
    whole = mask_v[...].astype(F32)
    low, high = whole[:blocks], whole[blocks:]
    swapped = sub != 0
    mine, theirs = jnp.where(swapped, high, low), jnp.where(swapped, low, high)
    mask[...] = jnp.concatenate([mine, theirs], axis=0).astype(BF16)
    for load in loads[2:4]:
        load.wait()
    own[half:, :] = padded_rows(mine)

    @pl.when(mon == 0)
    def _():
        for copy in part_copies:
            copy.wait_recv()
        far[half:, :] = padded_rows(far_mask[...].astype(F32))
        for copy in part_copies:
            copy.wait_send()


def order_rows(row, half, sub):
    flipped = jnp.where(row >= half, row - half, row + half)
    return jnp.where(row < 0, -1, jnp.where(sub == 0, row, flipped))


def spare_kernel(own, rest, mask, values, place, total_s, extra, spread):
    half, width = rest.shape
    capacity = extra.shape[1]
    groups = 2 * capacity // BLOCK
    sub = lax.axis_index("sub")
    extra[...] = jnp.zeros_like(extra)

    def one_lot(lot, carry):
        spread_lot(place, lot, groups, spread)
        row, column = wanted_of(values[...], spread[...])
        row = order_rows(row, half, sub)
        level = lax.broadcasted_iota(I32, (width, LOT), 0)
        hot = ones_where(level == column)
        found = found_of([own[0:half, :], rest[...]], mask[...], hot, row)
        cross = scatter(found, spread[...])
        extra[0:1, :] += cross[:, :capacity]
        extra[1:2, :] += cross[:, capacity:]
        return carry

    lax.fori_loop(1, (total_s[0] + LOT - 1) // LOT, one_lot, 0)


def main_kernel(n_mon, n_sub, chunk, own, first_far, rest, mask, pair_v, base_v, flow, hot, wanted, spread, extra, count_s,
                product, keep, shifts, base_wide,
                told, cross_got, flow_got, far, far_mask, cross_send, cross_recv, flow_send, flow_recv, part_send, part_recv):
    half, width = rest.shape
    blocks = half // BLOCK
    capacity = pair_v.shape[1]
    chunks = capacity // chunk
    n = n_mon * n_sub
    mon = lax.axis_index("mon")
    sub = lax.axis_index("sub")
    other = 1 - sub
    me = mon * n_sub + sub

    def peer(step):
        flat = lax.rem(me + step, n)
        return {"mon": flat // n_sub, "sub": lax.rem(flat, n_sub)}

    barrier = pltpu.get_barrier_semaphore()

    def greet(step, carry):
        pl.semaphore_signal(barrier, inc=1, device_id=peer(step), device_id_type=MESH)
        return carry

    lax.fori_loop(1, n, greet, 0)
    row = order_rows(wanted[...], half, sub)
    found = found_of([own[0:half, :], rest[...]], mask[...], hot[...], row)
    cross = scatter(found, spread[...])
    told[...] = stack_groups(cross + jnp.concatenate([extra[0:1, :], extra[1:2, :]], axis=1), told.shape[0]).astype(BF16)

    def hot_columns(c, side):
        span = pl.ds(pl.multiple_of(c * chunk, chunk), chunk)
        columns = jnp.concatenate([pair_v[0:1, span], pair_v[1:2, span]], axis=1) - side * width
        level = lax.broadcasted_iota(I32, (width, 2 * chunk), 0)
        return ones_where(level == columns)

    def make(far_ref):
        def one_chunk(c, carry):
            whole = jnp.concatenate([own[...], far_ref[...]], axis=1)
            columns = jnp.concatenate([hot_columns(c, sub), hot_columns(c, other)], axis=0)
            made = jnp.dot(whole, columns, preferred_element_type=F32)
            product[c] = made[:half].astype(product.dtype)
            keep[c] = made[half:half + blocks]
            return carry

        return one_chunk

    def near_chunk(c, carry):
        made = jnp.dot(own[...], hot_columns(c, sub), preferred_element_type=F32)
        product[c] = made[:half].astype(product.dtype)
        keep[c] = made[half:half + blocks]
        return carry

    def far_chunk(c, carry):
        made = jnp.dot(far[...], hot_columns(c, other), preferred_element_type=F32)
        product[c] = (product[c].astype(F32) + made[:half]).astype(product.dtype)
        keep[c] += made[half:half + blocks]
        return carry

    near_ahead = jnp.where(mon < n_mon // 2, chunks, jnp.where(mon == n_mon // 2, 1, 0))
    root = (lax.axis_index("grp") == 0) & (lax.axis_index("pair") == 0)
    ahead = jnp.where(root, chunks, 1)

    @pl.when(mon == 0)
    def _():
        lax.fori_loop(0, ahead, make(first_far), 0)

    @pl.when(mon != 0)
    def _():
        lax.fori_loop(0, near_ahead, near_chunk, 0)

    pl.semaphore_wait(barrier, n - 1)

    def send(step, carry):
        pltpu.make_async_remote_copy(
            told, cross_got.at[step - 1], cross_send, cross_recv, device_id=peer(step), device_id_type=MESH).start()
        return carry

    def send_flow(step, carry):
        pltpu.make_async_remote_copy(
            flow, flow_got.at[step - 1], flow_send, flow_recv,
            device_id={"mon": lax.rem(mon + step, n_mon)}, device_id_type=MESH).start()
        return carry

    lax.fori_loop(1, n, send, 0)
    lax.fori_loop(1, n_mon, send_flow, 0)
    partner = {"sub": other}
    part_copies = [
        pltpu.make_async_remote_copy(
            rest, far.at[pl.ds(0, half)],
            part_send.at[0], part_recv.at[0], device_id=partner, device_id_type=MESH),
        pltpu.make_async_remote_copy(
            mask, far_mask,
            part_send.at[1], part_recv.at[1], device_id=partner, device_id_type=MESH),
    ]

    @pl.when(mon != 0)
    def _():
        for copy in part_copies:
            copy.start()

    base = jnp.where(sub == 0, base_v[0:blocks], base_v[blocks:2 * blocks])
    for b in range(blocks):
        base_wide[b * BLOCK:(b + 1) * BLOCK, :] = jnp.broadcast_to(base[b:b + 1, :], (BLOCK, BLOCK)).T

    @pl.when(mon == 0)
    def _():
        lax.fori_loop(ahead, chunks, make(first_far), 0)

    @pl.when(mon != 0)
    def _():
        lax.fori_loop(near_ahead, chunks, near_chunk, 0)
        for copy in part_copies:
            copy.wait_recv()
        far[half:, :] = padded_rows(far_mask[...].astype(F32)[blocks:])
        lax.fori_loop(0, chunks, far_chunk, 0)
        for copy in part_copies:
            copy.wait_send()

    live = (lax.broadcasted_iota(I32, (1, capacity), 1) < count_s[0]).astype(F32)
    pltpu.make_async_copy(flow_got, flow_got, flow_recv).wait()
    flows = flow[...] + jnp.sum(flow_got[...], axis=0)
    pltpu.make_async_copy(cross_got, cross_got, cross_recv).wait()
    cross = told[...].astype(F32) + jnp.sum(cross_got[...].astype(F32), axis=0)
    rows = capacity // BLOCK
    cross_first, cross_second = cross[:rows], cross[rows:2 * rows]
    flow_first, flow_second = flows[:rows], flows[rows:2 * rows]
    determinant = 1.0 - cross_first * cross_second
    shift_first = ((flow_first + cross_first * flow_second) / determinant).astype(BF16).astype(F32)
    shift_second = ((flow_second + cross_second * flow_first) / determinant).astype(BF16).astype(F32)
    for g in range(rows):
        span = slice(g * BLOCK, (g + 1) * BLOCK)
        shifts[0:1, span] = shift_first[g:g + 1] * live[:, span]
        shifts[1:2, span] = shift_second[g:g + 1] * live[:, span]
    shifts[2:3, :] = live
    pltpu.make_async_copy(flow_got, flow_got, flow_send).wait()
    pltpu.make_async_copy(cross_got, cross_got, cross_send).wait()


def last_kernel(product, keep, shifts, base_wide, out_hbm, out_v, sems):
    chunks, half, pair_width = product.shape
    chunk = pair_width // 2
    copies = []
    for b in range(half // BLOCK):
        rows = slice(b * BLOCK, (b + 1) * BLOCK)
        flows = jnp.concatenate([base_wide[rows, :]] * (chunk // BLOCK), axis=1)
        for c in range(chunks):
            span = slice(c * chunk, (c + 1) * chunk)
            effect_first = shifts[0:1, span] * keep[c, b:b + 1, :chunk]
            effect_second = shifts[1:2, span] * keep[c, b:b + 1, chunk:]
            value = flows * shifts[2:3, span] + product[c, rows, :chunk] * effect_first
            value = value + product[c, rows, chunk:] * effect_second
            out_v[rows, span] = value.astype(BF16)
        place = pl.ds(b * BLOCK, BLOCK)
        copies.append(pltpu.make_async_copy(out_v.at[place], out_hbm.at[place], sems.at[b]))
        copies[-1].start()
    for copy in copies:
        copy.wait()


def on_device(n_mon, n_sub, dfactors, block_mask, base_flow, branch_row, pair_slots, pair_counts):
    rows_dev, width = dfactors.shape
    half = rows_dev // n_sub
    blocks = half // BLOCK
    tail = -(-blocks // 16) * 16
    capacity = pair_slots.shape[0]
    chunk = 256 if capacity % 256 == 0 else BLOCK
    chunks = capacity // chunk
    groups = 2 * capacity // BLOCK
    padded = -(-groups // 16) * 16
    n = n_mon * n_sub
    any_spec = pl.BlockSpec(memory_space=pltpu.HBM)
    vmem_spec = pl.BlockSpec(memory_space=pltpu.VMEM)
    smem_spec = pl.BlockSpec(memory_space=pltpu.SMEM)
    dma = pltpu.SemaphoreType.DMA

    def params(mib, **more):
        return pltpu.CompilerParams(vmem_limit_bytes=int(mib * 1024 * 1024), **more)

    def kept(arrays):
        return [pltpu.with_memory_space_constraint(array, pltpu.VMEM) for array in arrays]

    *made, total = pl.pallas_call(
        functools.partial(head_kernel, n_sub),
        out_shape=[
            pltpu.VMEM((half + tail, width), BF16),
            pltpu.VMEM((half + tail, width), BF16),
            pltpu.VMEM((half, width), BF16),
            pltpu.VMEM((n_sub * blocks, width), BF16),
            pltpu.VMEM((2, capacity), I32),
            pltpu.VMEM((n_sub * blocks, BLOCK), F32),
            pltpu.VMEM((padded, BLOCK), F32),
            pltpu.VMEM((8, 2 * capacity), BF16),
            pltpu.VMEM((padded, BLOCK), I32),
            pltpu.VMEM((width, LOT), BF16),
            pltpu.VMEM((1, LOT), I32),
            pltpu.VMEM((LOT, 2 * capacity), BF16),
            pltpu.SMEM((1,), I32),
        ],
        in_specs=[any_spec] * 5 + [smem_spec],
        out_specs=[vmem_spec] * 12 + [smem_spec],
        scratch_shapes=[
            pltpu.VMEM((branch_row.shape[0] // BLOCK, BLOCK), I32),
            pltpu.VMEM((n_sub * blocks, width), I32),
            pltpu.VMEM((blocks, width), I32),
            dma((6,)), dma((2,)), dma((2,)),
        ],
        compiler_params=params(58.8, collective_id=0, has_side_effects=True),
    )(dfactors, block_mask, base_flow.reshape(-1, BLOCK), branch_row.reshape(-1, BLOCK), pair_slots.T, pair_counts)
    own, far, rest, mask, pair_v, base_v, flow, values, place, hot, wanted, spread = kept(made)
    extra = pl.pallas_call(
        spare_kernel,
        out_shape=pltpu.VMEM((2, capacity), F32),
        in_specs=[vmem_spec] * 5 + [smem_spec],
        out_specs=vmem_spec,
        scratch_shapes=[pltpu.VMEM((LOT, 2 * capacity), BF16)],
        compiler_params=params(24),
    )(own, rest, mask, values, place, total)
    made = pl.pallas_call(
        functools.partial(main_kernel, n_mon, n_sub, chunk),
        out_shape=[
            pltpu.VMEM((chunks, half, 2 * chunk), F32),
            pltpu.VMEM((chunks, blocks, 2 * chunk), F32),
            pltpu.VMEM((3, capacity), F32),
            pltpu.VMEM((half, BLOCK), F32),
        ],
        in_specs=[vmem_spec] * 11 + [smem_spec],
        out_specs=[vmem_spec] * 4,
        scratch_shapes=[
            pltpu.VMEM((padded, BLOCK), BF16),
            pltpu.VMEM((n - 1, padded, BLOCK), BF16),
            pltpu.VMEM((n_mon - 1, padded, BLOCK), F32),
            pltpu.VMEM((half + tail, width), BF16),
            pltpu.VMEM((n_sub * blocks, width), BF16),
            dma, dma, dma, dma, dma((2,)), dma((2,)),
        ],
        compiler_params=params(40, collective_id=1, has_side_effects=True),
    )(own, far, rest, mask, pair_v, base_v, flow, hot, wanted, spread, kept([extra])[0], pair_counts)
    return pl.pallas_call(
        last_kernel,
        out_shape=jax.ShapeDtypeStruct((half, capacity), BF16),
        in_specs=[vmem_spec] * 4,
        out_specs=any_spec,
        scratch_shapes=[pltpu.VMEM((half, capacity), BF16), dma((blocks,))],
        compiler_params=params(16),
    )(*kept(made))


def solution(mesh):
    return jax.shard_map(
        functools.partial(on_device, mesh.shape["mon"], mesh.shape["sub"]),
        mesh=mesh,
        in_specs=(
            P("mon", "sub"),
            P("mon", "sub"),
            P("mon"),
            P(),
            P(("grp", "pair"), None),
            P(("grp", "pair")),
        ),
        out_specs=P(("mon", "sub"), ("grp", "pair")),
        check_vma=False,
    )
```

```python
import functools

import jax
import jax.numpy as jnp
from jax import lax
from jax.experimental import pallas as pl
from jax.experimental.pallas import tpu as pltpu
from jax.sharding import PartitionSpec as P

BLOCK = 128
LOT = 256
MESH = pl.DeviceIdType.MESH
F32 = jnp.float32
BF16 = jnp.bfloat16
I32 = jnp.int32


def lookup(table, index):
    groups = []
    height = table.shape[0]
    for start in range(0, index.shape[1], 128):
        wide = jnp.broadcast_to(index[:, start:start + 128], (height, 128))
        lanes = jnp.take_along_axis(table, wide & 127, axis=1)
        level = lax.broadcasted_iota(I32, (height, 128), 0)
        picked = jnp.where(level == (wide >> 7), lanes, jnp.zeros_like(lanes))
        groups.append(jnp.sum(picked, axis=0, keepdims=True))
    return jnp.concatenate(groups, axis=1)


def stack_groups(wide, height):
    rows = [wide[:, start:start + BLOCK] for start in range(0, wide.shape[1], BLOCK)]
    rows += [jnp.zeros((1, BLOCK), wide.dtype)] * (height - len(rows))
    return jnp.concatenate(rows, axis=0)


def ones_where(condition):
    return jnp.where(condition, F32(1), F32(0)).astype(BF16)


def spread_lot(place_ref, lot, groups, spread_ref):
    level = lax.broadcasted_iota(I32, (LOT, BLOCK), 0) + lot * LOT
    for g in range(groups):
        spread_ref[:, g * BLOCK:(g + 1) * BLOCK] = ones_where(level == place_ref[g:g + 1, :])


def wanted_of(values, spread):
    picked = lax.dot_general(values, spread, (((1,), (1,)), ((), ())), preferred_element_type=F32).astype(I32)
    filled = picked[4:5] > 0
    row = jnp.where(filled, picked[0:1] * 256 + picked[1:2], -1)
    column = jnp.where(filled, picked[2:3] * 256 + picked[3:4], -1)
    return row, column


def found_of(parts, mask, hot, row):
    found = jnp.zeros((1, LOT), F32)
    start = 0
    for part in parts:
        near = jnp.dot(part, hot, preferred_element_type=F32)
        level = lax.broadcasted_iota(I32, near.shape, 0) + start
        found = found + jnp.sum(jnp.where(level == row, near, F32(0)), axis=0, keepdims=True)
        start += part.shape[0]
    kept = jnp.dot(mask, hot, preferred_element_type=F32)
    level = lax.broadcasted_iota(I32, kept.shape, 0)
    return found * jnp.sum(jnp.where(level == (row >> 7), kept, F32(0)), axis=0, keepdims=True)


def scatter(found, spread):
    wide = jnp.broadcast_to(found, (8, LOT)).astype(BF16)
    return jnp.dot(wide, spread, preferred_element_type=F32)[0:1]


def padded_rows(rows):
    pad = jnp.zeros((-rows.shape[0] % 16, rows.shape[1]), F32)
    return jnp.concatenate([rows, pad], axis=0).astype(BF16)


def head_kernel(n_sub, df_hbm, mask_hbm, base_hbm, row_hbm, pair_hbm, count_s,
                own, far, rest, mask, pair_v, base_v, flow, values, place, hot, wanted, spread, total_s,
                row_v, mask_v, far_mask, load_sem, part_send, part_recv):
    rows_dev, width = df_hbm.shape
    half = rows_dev // n_sub
    blocks = half // BLOCK
    capacity = pair_hbm.shape[1]
    groups = 2 * capacity // BLOCK
    mon = lax.axis_index("mon")
    sub = lax.axis_index("sub")
    other = 1 - sub
    partner = {"sub": other}

    barrier = pltpu.get_barrier_semaphore()

    @pl.when(mon == 0)
    def _():
        pl.semaphore_signal(barrier, inc=1, device_id=partner, device_id_type=MESH)

    loads = [
        pltpu.make_async_copy(row_hbm, row_v, load_sem.at[0]),
        pltpu.make_async_copy(pair_hbm, pair_v, load_sem.at[1]),
        pltpu.make_async_copy(df_hbm.at[pl.ds(sub * half, half)], own.at[pl.ds(0, half)], load_sem.at[2]),
        pltpu.make_async_copy(df_hbm.at[pl.ds(other * half, half)], rest, load_sem.at[3]),
        pltpu.make_async_copy(mask_hbm, mask_v, load_sem.at[4]),
        pltpu.make_async_copy(base_hbm, base_v, load_sem.at[5]),
    ]
    for load in loads:
        load.start()
    part_copies = [
        pltpu.make_async_remote_copy(
            df_hbm.at[pl.ds(other * half, half)], far.at[pl.ds(0, half)],
            part_send.at[0], part_recv.at[0], device_id=partner, device_id_type=MESH),
        pltpu.make_async_remote_copy(
            mask_hbm.at[pl.ds(other * blocks, blocks)], far_mask,
            part_send.at[1], part_recv.at[1], device_id=partner, device_id_type=MESH),
    ]

    @pl.when(mon == 0)
    def _():
        pl.semaphore_wait(barrier, 1)
        for copy in part_copies:
            copy.start()

    loads[0].wait()
    loads[1].wait()
    table = row_v[...]
    first, second = pair_v[0:1, :], pair_v[1:2, :]
    first_row, second_row = lookup(table, first), lookup(table, second)
    row = jnp.concatenate([first_row, second_row], axis=1) - mon * rows_dev
    column = jnp.concatenate([second, first], axis=1) - sub * width
    slot = lax.broadcasted_iota(I32, (1, capacity), 1)
    live = slot < count_s[0]
    live = jnp.concatenate([live, live], axis=1)
    local = (row >= 0) & (row < rows_dev) & (column >= 0) & (column < width) & live
    flags = jnp.where(local, F32(1), F32(0))
    running = jnp.zeros((1, BLOCK), F32)
    flag_rows, before_rows = [], []
    for g in range(groups):
        flag_rows.append(flags[:, g * BLOCK:(g + 1) * BLOCK])
        before_rows.append(running)
        running = running + flag_rows[-1]
    padding = [jnp.zeros((1, BLOCK), F32)] * (place.shape[0] - groups)
    flag_grid = jnp.concatenate(flag_rows + padding, axis=0)
    counted = jnp.concatenate([flag_grid, jnp.concatenate(before_rows + padding, axis=0)], axis=1)
    across = lax.broadcasted_iota(I32, (2 * BLOCK, BLOCK), 0)
    down = lax.broadcasted_iota(I32, (2 * BLOCK, BLOCK), 1)
    adder = ones_where((across < down) | (across >= BLOCK))
    order = jnp.dot(counted.astype(BF16), adder, preferred_element_type=F32).astype(I32)
    place[...] = jnp.where(flag_grid > 0, order, -1)
    zero = jnp.zeros_like(row)
    stacked = jnp.concatenate([row >> 8, row & 255, column >> 8, column & 255, zero + 1, zero, zero, zero], axis=0)
    values[...] = stacked.astype(F32).astype(BF16)
    spread_lot(place, 0, groups, spread)
    wanted_row, wanted_column = wanted_of(values[...], spread[...])
    wanted[...] = wanted_row
    level = lax.broadcasted_iota(I32, (width, LOT), 0)
    hot[...] = ones_where(level == wanted_column)
    total_s[0] = jnp.sum(running).astype(I32)

    loads[5].wait()
    base = base_v[...]
    flow[...] = stack_groups(lookup(base, row), flow.shape[0])
    loads[4].wait()
    whole = mask_v[...].astype(F32)
    low, high = whole[:blocks], whole[blocks:]
    swapped = sub != 0
    mine, theirs = jnp.where(swapped, high, low), jnp.where(swapped, low, high)
    mask[...] = jnp.concatenate([mine, theirs], axis=0).astype(BF16)
    for load in loads[2:4]:
        load.wait()
    own[half:, :] = padded_rows(mine)

    @pl.when(mon == 0)
    def _():
        for copy in part_copies:
            copy.wait_recv()
        far[half:, :] = padded_rows(far_mask[...].astype(F32))
        for copy in part_copies:
            copy.wait_send()


def order_rows(row, half, sub):
    flipped = jnp.where(row >= half, row - half, row + half)
    return jnp.where(row < 0, -1, jnp.where(sub == 0, row, flipped))


def spare_kernel(own, rest, mask, values, place, total_s, extra, spread):
    half, width = rest.shape
    capacity = extra.shape[1]
    groups = 2 * capacity // BLOCK
    sub = lax.axis_index("sub")
    extra[...] = jnp.zeros_like(extra)

    def one_lot(lot, carry):
        spread_lot(place, lot, groups, spread)
        row, column = wanted_of(values[...], spread[...])
        row = order_rows(row, half, sub)
        level = lax.broadcasted_iota(I32, (width, LOT), 0)
        hot = ones_where(level == column)
        found = found_of([own[0:half, :], rest[...]], mask[...], hot, row)
        cross = scatter(found, spread[...])
        extra[0:1, :] += cross[:, :capacity]
        extra[1:2, :] += cross[:, capacity:]
        return carry

    lax.fori_loop(1, (total_s[0] + LOT - 1) // LOT, one_lot, 0)


def main_kernel(n_mon, n_sub, chunk, own, first_far, rest, mask, pair_v, base_v, flow, hot, wanted, spread, extra, count_s,
                product, keep, shifts, base_wide,
                told, cross_got, flow_got, far, far_mask, cross_send, cross_recv, flow_send, flow_recv, part_send, part_recv):
    half, width = rest.shape
    blocks = half // BLOCK
    capacity = pair_v.shape[1]
    chunks = capacity // chunk
    n = n_mon * n_sub
    mon = lax.axis_index("mon")
    sub = lax.axis_index("sub")
    other = 1 - sub
    me = mon * n_sub + sub

    def peer(step):
        flat = lax.rem(me + step, n)
        return {"mon": flat // n_sub, "sub": lax.rem(flat, n_sub)}

    barrier = pltpu.get_barrier_semaphore()

    def greet(step, carry):
        pl.semaphore_signal(barrier, inc=1, device_id=peer(step), device_id_type=MESH)
        return carry

    lax.fori_loop(1, n, greet, 0)
    row = order_rows(wanted[...], half, sub)
    found = found_of([own[0:half, :], rest[...]], mask[...], hot[...], row)
    cross = scatter(found, spread[...])
    told[...] = stack_groups(cross + jnp.concatenate([extra[0:1, :], extra[1:2, :]], axis=1), told.shape[0]).astype(BF16)

    def hot_columns(c, side):
        span = pl.ds(c * chunk if isinstance(c, int) else pl.multiple_of(c * chunk, chunk), chunk)
        columns = jnp.concatenate([pair_v[0:1, span], pair_v[1:2, span]], axis=1) - side * width
        level = lax.broadcasted_iota(I32, (width, 2 * chunk), 0)
        return ones_where(level == columns)

    def make(far_ref):
        def one_chunk(c, carry):
            whole = jnp.concatenate([own[...], far_ref[...]], axis=1)
            columns = jnp.concatenate([hot_columns(c, sub), hot_columns(c, other)], axis=0)
            made = jnp.dot(whole, columns, preferred_element_type=F32)
            product[c] = made[:half].astype(product.dtype)
            keep[c] = made[half:half + blocks]
            return carry

        return one_chunk

    def near_chunk(c, carry):
        made = jnp.dot(own[...], hot_columns(c, sub), preferred_element_type=F32)
        product[c] = made[:half].astype(product.dtype)
        keep[c] = made[half:half + blocks]
        return carry

    def far_chunk(c, carry):
        made = jnp.dot(far[...], hot_columns(c, other), preferred_element_type=F32)
        product[c] = (product[c].astype(F32) + made[:half]).astype(product.dtype)
        keep[c] += made[half:half + blocks]
        return carry

    early = mon < n_mon // 2
    root = (lax.axis_index("grp") == 0) & (lax.axis_index("pair") == 0)
    ahead = jnp.where(root, chunks, 1)

    @pl.when(mon == 0)
    def _():
        lax.fori_loop(0, ahead, make(first_far), 0)

    @pl.when((mon != 0) & early)
    def _():
        for c in range(chunks):
            near_chunk(c, 0)

    pl.semaphore_wait(barrier, n - 1)

    def send(step, carry):
        pltpu.make_async_remote_copy(
            told, cross_got.at[step - 1], cross_send, cross_recv, device_id=peer(step), device_id_type=MESH).start()
        return carry

    def send_flow(step, carry):
        pltpu.make_async_remote_copy(
            flow, flow_got.at[step - 1], flow_send, flow_recv,
            device_id={"mon": lax.rem(mon + step, n_mon)}, device_id_type=MESH).start()
        return carry

    lax.fori_loop(1, n, send, 0)
    lax.fori_loop(1, n_mon, send_flow, 0)
    partner = {"sub": other}
    part_copies = [
        pltpu.make_async_remote_copy(
            rest, far.at[pl.ds(0, half)],
            part_send.at[0], part_recv.at[0], device_id=partner, device_id_type=MESH),
        pltpu.make_async_remote_copy(
            mask, far_mask,
            part_send.at[1], part_recv.at[1], device_id=partner, device_id_type=MESH),
    ]

    @pl.when(mon != 0)
    def _():
        for copy in part_copies:
            copy.start()

    base = jnp.where(sub == 0, base_v[0:blocks], base_v[blocks:2 * blocks])
    for b in range(blocks):
        base_wide[b * BLOCK:(b + 1) * BLOCK, :] = jnp.broadcast_to(base[b:b + 1, :], (BLOCK, BLOCK)).T

    @pl.when(mon == 0)
    def _():
        lax.fori_loop(ahead, chunks, make(first_far), 0)

    @pl.when(jnp.logical_not(early))
    def _():
        for c in range(chunks):
            near_chunk(c, 0)

    @pl.when(mon != 0)
    def _():
        for copy in part_copies:
            copy.wait_recv()
        far[half:, :] = padded_rows(far_mask[...].astype(F32)[blocks:])
        for c in range(chunks):
            far_chunk(c, 0)
        for copy in part_copies:
            copy.wait_send()

    live = (lax.broadcasted_iota(I32, (1, capacity), 1) < count_s[0]).astype(F32)
    pltpu.make_async_copy(flow_got, flow_got, flow_recv).wait()
    flows = flow[...] + jnp.sum(flow_got[...], axis=0)
    pltpu.make_async_copy(cross_got, cross_got, cross_recv).wait()
    cross = told[...].astype(F32) + jnp.sum(cross_got[...].astype(F32), axis=0)
    rows = capacity // BLOCK
    cross_first, cross_second = cross[:rows], cross[rows:2 * rows]
    flow_first, flow_second = flows[:rows], flows[rows:2 * rows]
    determinant = 1.0 - cross_first * cross_second
    shift_first = ((flow_first + cross_first * flow_second) / determinant).astype(BF16).astype(F32)
    shift_second = ((flow_second + cross_second * flow_first) / determinant).astype(BF16).astype(F32)
    for g in range(rows):
        span = slice(g * BLOCK, (g + 1) * BLOCK)
        shifts[0:1, span] = shift_first[g:g + 1] * live[:, span]
        shifts[1:2, span] = shift_second[g:g + 1] * live[:, span]
    shifts[2:3, :] = live
    pltpu.make_async_copy(flow_got, flow_got, flow_send).wait()
    pltpu.make_async_copy(cross_got, cross_got, cross_send).wait()


def last_kernel(product, keep, shifts, base_wide, out_hbm, out_v, sems):
    chunks, half, pair_width = product.shape
    chunk = pair_width // 2
    copies = []
    for b in range(half // BLOCK):
        rows = slice(b * BLOCK, (b + 1) * BLOCK)
        flows = jnp.concatenate([base_wide[rows, :]] * (chunk // BLOCK), axis=1)
        for c in range(chunks):
            span = slice(c * chunk, (c + 1) * chunk)
            effect_first = shifts[0:1, span] * keep[c, b:b + 1, :chunk]
            effect_second = shifts[1:2, span] * keep[c, b:b + 1, chunk:]
            value = flows * shifts[2:3, span] + product[c, rows, :chunk] * effect_first
            value = value + product[c, rows, chunk:] * effect_second
            out_v[rows, span] = value.astype(BF16)
        place = pl.ds(b * BLOCK, BLOCK)
        copies.append(pltpu.make_async_copy(out_v.at[place], out_hbm.at[place], sems.at[b]))
        copies[-1].start()
    for copy in copies:
        copy.wait()


def on_device(n_mon, n_sub, dfactors, block_mask, base_flow, branch_row, pair_slots, pair_counts):
    rows_dev, width = dfactors.shape
    half = rows_dev // n_sub
    blocks = half // BLOCK
    tail = -(-blocks // 16) * 16
    capacity = pair_slots.shape[0]
    chunk = 256 if capacity % 256 == 0 else BLOCK
    chunks = capacity // chunk
    groups = 2 * capacity // BLOCK
    padded = -(-groups // 16) * 16
    n = n_mon * n_sub
    any_spec = pl.BlockSpec(memory_space=pltpu.HBM)
    vmem_spec = pl.BlockSpec(memory_space=pltpu.VMEM)
    smem_spec = pl.BlockSpec(memory_space=pltpu.SMEM)
    dma = pltpu.SemaphoreType.DMA

    def params(mib, **more):
        return pltpu.CompilerParams(vmem_limit_bytes=int(mib * 1024 * 1024), **more)

    def kept(arrays):
        return [pltpu.with_memory_space_constraint(array, pltpu.VMEM) for array in arrays]

    *made, total = pl.pallas_call(
        functools.partial(head_kernel, n_sub),
        out_shape=[
            pltpu.VMEM((half + tail, width), BF16),
            pltpu.VMEM((half + tail, width), BF16),
            pltpu.VMEM((half, width), BF16),
            pltpu.VMEM((n_sub * blocks, width), BF16),
            pltpu.VMEM((2, capacity), I32),
            pltpu.VMEM((n_sub * blocks, BLOCK), F32),
            pltpu.VMEM((padded, BLOCK), F32),
            pltpu.VMEM((8, 2 * capacity), BF16),
            pltpu.VMEM((padded, BLOCK), I32),
            pltpu.VMEM((width, LOT), BF16),
            pltpu.VMEM((1, LOT), I32),
            pltpu.VMEM((LOT, 2 * capacity), BF16),
            pltpu.SMEM((1,), I32),
        ],
        in_specs=[any_spec] * 5 + [smem_spec],
        out_specs=[vmem_spec] * 12 + [smem_spec],
        scratch_shapes=[
            pltpu.VMEM((branch_row.shape[0] // BLOCK, BLOCK), I32),
            pltpu.VMEM((n_sub * blocks, width), I32),
            pltpu.VMEM((blocks, width), I32),
            dma((6,)), dma((2,)), dma((2,)),
        ],
        compiler_params=params(58.8, collective_id=0, has_side_effects=True),
    )(dfactors, block_mask, base_flow.reshape(-1, BLOCK), branch_row.reshape(-1, BLOCK), pair_slots.T, pair_counts)
    own, far, rest, mask, pair_v, base_v, flow, values, place, hot, wanted, spread = kept(made)
    extra = pl.pallas_call(
        spare_kernel,
        out_shape=pltpu.VMEM((2, capacity), F32),
        in_specs=[vmem_spec] * 5 + [smem_spec],
        out_specs=vmem_spec,
        scratch_shapes=[pltpu.VMEM((LOT, 2 * capacity), BF16)],
        compiler_params=params(24),
    )(own, rest, mask, values, place, total)
    made = pl.pallas_call(
        functools.partial(main_kernel, n_mon, n_sub, chunk),
        out_shape=[
            pltpu.VMEM((chunks, half, 2 * chunk), F32),
            pltpu.VMEM((chunks, blocks, 2 * chunk), F32),
            pltpu.VMEM((3, capacity), F32),
            pltpu.VMEM((half, BLOCK), F32),
        ],
        in_specs=[vmem_spec] * 11 + [smem_spec],
        out_specs=[vmem_spec] * 4,
        scratch_shapes=[
            pltpu.VMEM((padded, BLOCK), BF16),
            pltpu.VMEM((n - 1, padded, BLOCK), BF16),
            pltpu.VMEM((n_mon - 1, padded, BLOCK), F32),
            pltpu.VMEM((half + tail, width), BF16),
            pltpu.VMEM((n_sub * blocks, width), BF16),
            dma, dma, dma, dma, dma((2,)), dma((2,)),
        ],
        compiler_params=params(40, collective_id=1, has_side_effects=True),
    )(own, far, rest, mask, pair_v, base_v, flow, hot, wanted, spread, kept([extra])[0], pair_counts)
    return pl.pallas_call(
        last_kernel,
        out_shape=jax.ShapeDtypeStruct((half, capacity), BF16),
        in_specs=[vmem_spec] * 4,
        out_specs=any_spec,
        scratch_shapes=[pltpu.VMEM((half, capacity), BF16), dma((blocks,))],
        compiler_params=params(16),
    )(*kept(made))


def solution(mesh):
    return jax.shard_map(
        functools.partial(on_device, mesh.shape["mon"], mesh.shape["sub"]),
        mesh=mesh,
        in_specs=(
            P("mon", "sub"),
            P("mon", "sub"),
            P("mon"),
            P(),
            P(("grp", "pair"), None),
            P(("grp", "pair")),
        ),
        out_specs=P(("mon", "sub"), ("grp", "pair")),
        check_vma=False,
    )
```

```python
import functools

import jax
import jax.numpy as jnp
from jax import lax
from jax.experimental import pallas as pl
from jax.experimental.pallas import tpu as pltpu
from jax.sharding import PartitionSpec as P

BLOCK = 128
LOT = 256
MESH = pl.DeviceIdType.MESH
F32 = jnp.float32
BF16 = jnp.bfloat16
I32 = jnp.int32


def lookup(table, index):
    groups = []
    height = table.shape[0]
    for start in range(0, index.shape[1], 128):
        wide = jnp.broadcast_to(index[:, start:start + 128], (height, 128))
        lanes = jnp.take_along_axis(table, wide & 127, axis=1)
        level = lax.broadcasted_iota(I32, (height, 128), 0)
        picked = jnp.where(level == (wide >> 7), lanes, jnp.zeros_like(lanes))
        groups.append(jnp.sum(picked, axis=0, keepdims=True))
    return jnp.concatenate(groups, axis=1)


def stack_groups(wide, height):
    rows = [wide[:, start:start + BLOCK] for start in range(0, wide.shape[1], BLOCK)]
    rows += [jnp.zeros((1, BLOCK), wide.dtype)] * (height - len(rows))
    return jnp.concatenate(rows, axis=0)


def ones_where(condition):
    return jnp.where(condition, F32(1), F32(0)).astype(BF16)


def spread_lot(place_ref, lot, groups, spread_ref):
    level = lax.broadcasted_iota(I32, (LOT, BLOCK), 0) + lot * LOT
    for g in range(groups):
        spread_ref[:, g * BLOCK:(g + 1) * BLOCK] = ones_where(level == place_ref[g:g + 1, :])


def wanted_of(values, spread):
    picked = lax.dot_general(values, spread, (((1,), (1,)), ((), ())), preferred_element_type=F32).astype(I32)
    filled = picked[4:5] > 0
    row = jnp.where(filled, picked[0:1] * 256 + picked[1:2], -1)
    column = jnp.where(filled, picked[2:3] * 256 + picked[3:4], -1)
    return row, column


def found_of(parts, mask, hot, row):
    found = jnp.zeros((1, LOT), F32)
    start = 0
    for part in parts:
        near = jnp.dot(part, hot, preferred_element_type=F32)
        level = lax.broadcasted_iota(I32, near.shape, 0) + start
        found = found + jnp.sum(jnp.where(level == row, near, F32(0)), axis=0, keepdims=True)
        start += part.shape[0]
    kept = jnp.dot(mask, hot, preferred_element_type=F32)
    level = lax.broadcasted_iota(I32, kept.shape, 0)
    return found * jnp.sum(jnp.where(level == (row >> 7), kept, F32(0)), axis=0, keepdims=True)


def scatter(found, place):
    lanes, level = place & (BLOCK - 1), place >> 7
    value = jnp.zeros(place.shape, F32)
    for t in range(LOT // BLOCK):
        wide = jnp.broadcast_to(found[:, t * BLOCK:(t + 1) * BLOCK], place.shape)
        value = value + jnp.where(level == t, jnp.take_along_axis(wide, lanes, axis=1), F32(0))
    return value


def padded_rows(rows):
    pad = jnp.zeros((-rows.shape[0] % 16, rows.shape[1]), F32)
    return jnp.concatenate([rows, pad], axis=0).astype(BF16)


def head_kernel(n_sub, df_hbm, mask_hbm, base_hbm, row_hbm, pair_hbm, count_s,
                own, far, rest, mask, pair_v, base_v, flow, values, place, hot, wanted, total_s,
                row_v, spread, mask_v, far_mask, load_sem, part_send, part_recv):
    rows_dev, width = df_hbm.shape
    half = rows_dev // n_sub
    blocks = half // BLOCK
    capacity = pair_hbm.shape[1]
    groups = 2 * capacity // BLOCK
    mon = lax.axis_index("mon")
    sub = lax.axis_index("sub")
    other = 1 - sub
    partner = {"sub": other}

    barrier = pltpu.get_barrier_semaphore()

    @pl.when(mon == 0)
    def _():
        pl.semaphore_signal(barrier, inc=1, device_id=partner, device_id_type=MESH)

    loads = [
        pltpu.make_async_copy(row_hbm, row_v, load_sem.at[0]),
        pltpu.make_async_copy(pair_hbm, pair_v, load_sem.at[1]),
        pltpu.make_async_copy(df_hbm.at[pl.ds(sub * half, half)], own.at[pl.ds(0, half)], load_sem.at[2]),
        pltpu.make_async_copy(df_hbm.at[pl.ds(other * half, half)], rest, load_sem.at[3]),
        pltpu.make_async_copy(mask_hbm, mask_v, load_sem.at[4]),
        pltpu.make_async_copy(base_hbm, base_v, load_sem.at[5]),
    ]
    for load in loads:
        load.start()
    part_copies = [
        pltpu.make_async_remote_copy(
            df_hbm.at[pl.ds(other * half, half)], far.at[pl.ds(0, half)],
            part_send.at[0], part_recv.at[0], device_id=partner, device_id_type=MESH),
        pltpu.make_async_remote_copy(
            mask_hbm.at[pl.ds(other * blocks, blocks)], far_mask,
            part_send.at[1], part_recv.at[1], device_id=partner, device_id_type=MESH),
    ]

    @pl.when(mon == 0)
    def _():
        pl.semaphore_wait(barrier, 1)
        for copy in part_copies:
            copy.start()

    loads[0].wait()
    loads[1].wait()
    table = row_v[...]
    first, second = pair_v[0:1, :], pair_v[1:2, :]
    first_row, second_row = lookup(table, first), lookup(table, second)
    row = jnp.concatenate([first_row, second_row], axis=1) - mon * rows_dev
    column = jnp.concatenate([second, first], axis=1) - sub * width
    slot = lax.broadcasted_iota(I32, (1, capacity), 1)
    live = slot < count_s[0]
    live = jnp.concatenate([live, live], axis=1)
    local = (row >= 0) & (row < rows_dev) & (column >= 0) & (column < width) & live
    flags = jnp.where(local, F32(1), F32(0))
    running = jnp.zeros((1, BLOCK), F32)
    flag_rows, before_rows = [], []
    for g in range(groups):
        flag_rows.append(flags[:, g * BLOCK:(g + 1) * BLOCK])
        before_rows.append(running)
        running = running + flag_rows[-1]
    padding = [jnp.zeros((1, BLOCK), F32)] * (place.shape[0] - groups)
    flag_grid = jnp.concatenate(flag_rows + padding, axis=0)
    counted = jnp.concatenate([flag_grid, jnp.concatenate(before_rows + padding, axis=0)], axis=1)
    across = lax.broadcasted_iota(I32, (2 * BLOCK, BLOCK), 0)
    down = lax.broadcasted_iota(I32, (2 * BLOCK, BLOCK), 1)
    adder = ones_where((across < down) | (across >= BLOCK))
    order = jnp.dot(counted.astype(BF16), adder, preferred_element_type=F32).astype(I32)
    place[...] = jnp.where(flag_grid > 0, order, -1)
    zero = jnp.zeros_like(row)
    stacked = jnp.concatenate([row >> 8, row & 255, column >> 8, column & 255, zero + 1, zero, zero, zero], axis=0)
    values[...] = stacked.astype(F32).astype(BF16)
    spread_lot(place, 0, groups, spread)
    wanted_row, wanted_column = wanted_of(values[...], spread[...])
    wanted[...] = wanted_row
    level = lax.broadcasted_iota(I32, (width, LOT), 0)
    hot[...] = ones_where(level == wanted_column)
    total_s[0] = jnp.sum(running).astype(I32)

    loads[5].wait()
    base = base_v[...]
    flow[...] = stack_groups(lookup(base, row), flow.shape[0])
    loads[4].wait()
    whole = mask_v[...].astype(F32)
    low, high = whole[:blocks], whole[blocks:]
    swapped = sub != 0
    mine, theirs = jnp.where(swapped, high, low), jnp.where(swapped, low, high)
    mask[...] = jnp.concatenate([mine, theirs], axis=0).astype(BF16)
    for load in loads[2:4]:
        load.wait()
    own[half:, :] = padded_rows(mine)

    @pl.when(mon == 0)
    def _():
        for copy in part_copies:
            copy.wait_recv()
        far[half:, :] = padded_rows(far_mask[...].astype(F32))
        for copy in part_copies:
            copy.wait_send()


def order_rows(row, half, sub):
    flipped = jnp.where(row >= half, row - half, row + half)
    return jnp.where(row < 0, -1, jnp.where(sub == 0, row, flipped))


def spare_kernel(own, rest, mask, values, place, total_s, extra, spread):
    half, width = rest.shape
    groups = values.shape[1] // BLOCK
    sub = lax.axis_index("sub")
    extra[...] = jnp.zeros_like(extra)

    def one_lot(lot, carry):
        spread_lot(place, lot, groups, spread)
        row, column = wanted_of(values[...], spread[...])
        row = order_rows(row, half, sub)
        level = lax.broadcasted_iota(I32, (width, LOT), 0)
        hot = ones_where(level == column)
        found = found_of([own[0:half, :], rest[...]], mask[...], hot, row)
        extra[...] += scatter(found, place[...] - lot * LOT)
        return carry

    lax.fori_loop(1, (total_s[0] + LOT - 1) // LOT, one_lot, 0)


def main_kernel(n_mon, n_sub, chunk, own, first_far, rest, mask, pair_v, base_v, flow, hot, wanted, place, extra, count_s,
                product, keep, shifts, base_wide,
                told, cross_got, flow_got, far, far_mask, cross_send, cross_recv, flow_send, flow_recv, part_send, part_recv):
    half, width = rest.shape
    blocks = half // BLOCK
    capacity = pair_v.shape[1]
    chunks = capacity // chunk
    n = n_mon * n_sub
    mon = lax.axis_index("mon")
    sub = lax.axis_index("sub")
    other = 1 - sub
    me = mon * n_sub + sub

    def peer(step):
        flat = lax.rem(me + step, n)
        return {"mon": flat // n_sub, "sub": lax.rem(flat, n_sub)}

    barrier = pltpu.get_barrier_semaphore()

    def greet(step, carry):
        pl.semaphore_signal(barrier, inc=1, device_id=peer(step), device_id_type=MESH)
        return carry

    lax.fori_loop(1, n, greet, 0)
    row = order_rows(wanted[...], half, sub)
    found = found_of([own[0:half, :], rest[...]], mask[...], hot[...], row)

    def tell():
        told[...] = (scatter(found, place[...]) + extra[...]).astype(BF16)

    late = mon > n_mon // 2

    @pl.when(jnp.logical_not(late))
    def _():
        tell()

    def hot_columns(c, side):
        span = pl.ds(c * chunk if isinstance(c, int) else pl.multiple_of(c * chunk, chunk), chunk)
        columns = jnp.concatenate([pair_v[0:1, span], pair_v[1:2, span]], axis=1) - side * width
        level = lax.broadcasted_iota(I32, (width, 2 * chunk), 0)
        return ones_where(level == columns)

    def make(far_ref):
        def one_chunk(c, carry):
            whole = jnp.concatenate([own[...], far_ref[...]], axis=1)
            columns = jnp.concatenate([hot_columns(c, sub), hot_columns(c, other)], axis=0)
            made = jnp.dot(whole, columns, preferred_element_type=F32)
            product[c] = made[:half].astype(product.dtype)
            keep[c] = made[half:half + blocks]
            return carry

        return one_chunk

    def near_chunk(c, carry):
        made = jnp.dot(own[...], hot_columns(c, sub), preferred_element_type=F32)
        product[c] = made[:half].astype(product.dtype)
        keep[c] = made[half:half + blocks]
        return carry

    def far_chunk(c, carry):
        made = jnp.dot(far[...], hot_columns(c, other), preferred_element_type=F32)
        product[c] = (product[c].astype(F32) + made[:half]).astype(product.dtype)
        keep[c] += made[half:half + blocks]
        return carry

    early = mon < n_mon // 2
    root = (lax.axis_index("grp") == 0) & (lax.axis_index("pair") == 0)
    ahead = jnp.where(root, chunks, 1)

    @pl.when(mon == 0)
    def _():
        lax.fori_loop(0, ahead, make(first_far), 0)

    @pl.when((mon != 0) & early)
    def _():
        for c in range(chunks):
            near_chunk(c, 0)

    pl.semaphore_wait(barrier, n - 1)

    def send_flow(i, carry):
        to = i + (i >= mon).astype(I32)
        pltpu.make_async_remote_copy(
            flow, flow_got.at[lax.rem(to + n_mon - mon, n_mon) - 1], flow_send, flow_recv,
            device_id={"mon": to}, device_id_type=MESH).start()
        return carry

    def send(i, carry):
        to = i + (i >= me).astype(I32)
        pltpu.make_async_remote_copy(
            told, cross_got.at[lax.rem(to + n - me, n) - 1], cross_send, cross_recv,
            device_id={"mon": to // n_sub, "sub": lax.rem(to, n_sub)}, device_id_type=MESH).start()
        return carry

    lax.fori_loop(0, n_mon - 1, send_flow, 0)

    @pl.when(late)
    def _():
        tell()

    lax.fori_loop(0, n - 1, send, 0)
    partner = {"sub": other}
    part_copies = [
        pltpu.make_async_remote_copy(
            rest, far.at[pl.ds(0, half)],
            part_send.at[0], part_recv.at[0], device_id=partner, device_id_type=MESH),
        pltpu.make_async_remote_copy(
            mask, far_mask,
            part_send.at[1], part_recv.at[1], device_id=partner, device_id_type=MESH),
    ]

    @pl.when(mon != 0)
    def _():
        for copy in part_copies:
            copy.start()

    base = jnp.where(sub == 0, base_v[0:blocks], base_v[blocks:2 * blocks])
    for b in range(blocks):
        base_wide[b * BLOCK:(b + 1) * BLOCK, :] = jnp.broadcast_to(base[b:b + 1, :], (BLOCK, BLOCK)).T

    @pl.when(mon == 0)
    def _():
        lax.fori_loop(ahead, chunks, make(first_far), 0)

    @pl.when(jnp.logical_not(early))
    def _():
        for c in range(chunks):
            near_chunk(c, 0)

    @pl.when(mon != 0)
    def _():
        for copy in part_copies:
            copy.wait_recv()
        far[half:, :] = padded_rows(far_mask[...].astype(F32)[blocks:])
        for c in range(chunks):
            far_chunk(c, 0)
        for copy in part_copies:
            copy.wait_send()

    live = (lax.broadcasted_iota(I32, (1, capacity), 1) < count_s[0]).astype(F32)
    pltpu.make_async_copy(flow_got, flow_got, flow_recv).wait()
    flows = flow[...] + jnp.sum(flow_got[...], axis=0)
    pltpu.make_async_copy(cross_got, cross_got, cross_recv).wait()
    cross = told[...].astype(F32) + jnp.sum(cross_got[...].astype(F32), axis=0)
    rows = capacity // BLOCK
    cross_first, cross_second = cross[:rows], cross[rows:2 * rows]
    flow_first, flow_second = flows[:rows], flows[rows:2 * rows]
    determinant = 1.0 - cross_first * cross_second
    shift_first = ((flow_first + cross_first * flow_second) / determinant).astype(BF16).astype(F32)
    shift_second = ((flow_second + cross_second * flow_first) / determinant).astype(BF16).astype(F32)
    for g in range(rows):
        span = slice(g * BLOCK, (g + 1) * BLOCK)
        shifts[0:1, span] = shift_first[g:g + 1] * live[:, span]
        shifts[1:2, span] = shift_second[g:g + 1] * live[:, span]
    shifts[2:3, :] = live
    pltpu.make_async_copy(flow_got, flow_got, flow_send).wait()
    pltpu.make_async_copy(cross_got, cross_got, cross_send).wait()


def last_kernel(product, keep, shifts, base_wide, out_hbm, out_v, sems):
    chunks, half, pair_width = product.shape
    chunk = pair_width // 2
    copies = []
    for b in range(half // BLOCK):
        rows = slice(b * BLOCK, (b + 1) * BLOCK)
        flows = jnp.concatenate([base_wide[rows, :]] * (chunk // BLOCK), axis=1)
        for c in range(chunks):
            span = slice(c * chunk, (c + 1) * chunk)
            effect_first = shifts[0:1, span] * keep[c, b:b + 1, :chunk]
            effect_second = shifts[1:2, span] * keep[c, b:b + 1, chunk:]
            value = flows * shifts[2:3, span] + product[c, rows, :chunk] * effect_first
            value = value + product[c, rows, chunk:] * effect_second
            out_v[rows, span] = value.astype(BF16)
        place = pl.ds(b * BLOCK, BLOCK)
        copies.append(pltpu.make_async_copy(out_v.at[place], out_hbm.at[place], sems.at[b]))
        copies[-1].start()
    for copy in copies:
        copy.wait()


def on_device(n_mon, n_sub, dfactors, block_mask, base_flow, branch_row, pair_slots, pair_counts):
    rows_dev, width = dfactors.shape
    half = rows_dev // n_sub
    blocks = half // BLOCK
    tail = -(-blocks // 16) * 16
    capacity = pair_slots.shape[0]
    chunk = 256 if capacity % 256 == 0 else BLOCK
    chunks = capacity // chunk
    groups = 2 * capacity // BLOCK
    padded = -(-groups // 16) * 16
    n = n_mon * n_sub
    any_spec = pl.BlockSpec(memory_space=pltpu.HBM)
    vmem_spec = pl.BlockSpec(memory_space=pltpu.VMEM)
    smem_spec = pl.BlockSpec(memory_space=pltpu.SMEM)
    dma = pltpu.SemaphoreType.DMA

    def params(mib, **more):
        return pltpu.CompilerParams(vmem_limit_bytes=int(mib * 1024 * 1024), **more)

    def kept(arrays):
        return [pltpu.with_memory_space_constraint(array, pltpu.VMEM) for array in arrays]

    *made, total = pl.pallas_call(
        functools.partial(head_kernel, n_sub),
        out_shape=[
            pltpu.VMEM((half + tail, width), BF16),
            pltpu.VMEM((half + tail, width), BF16),
            pltpu.VMEM((half, width), BF16),
            pltpu.VMEM((n_sub * blocks, width), BF16),
            pltpu.VMEM((2, capacity), I32),
            pltpu.VMEM((n_sub * blocks, BLOCK), F32),
            pltpu.VMEM((padded, BLOCK), F32),
            pltpu.VMEM((8, 2 * capacity), BF16),
            pltpu.VMEM((padded, BLOCK), I32),
            pltpu.VMEM((width, LOT), BF16),
            pltpu.VMEM((1, LOT), I32),
            pltpu.SMEM((1,), I32),
        ],
        in_specs=[any_spec] * 5 + [smem_spec],
        out_specs=[vmem_spec] * 11 + [smem_spec],
        scratch_shapes=[
            pltpu.VMEM((branch_row.shape[0] // BLOCK, BLOCK), I32),
            pltpu.VMEM((LOT, 2 * capacity), BF16),
            pltpu.VMEM((n_sub * blocks, width), I32),
            pltpu.VMEM((blocks, width), I32),
            dma((6,)), dma((2,)), dma((2,)),
        ],
        compiler_params=params(58.8, collective_id=0, has_side_effects=True),
    )(dfactors, block_mask, base_flow.reshape(-1, BLOCK), branch_row.reshape(-1, BLOCK), pair_slots.T, pair_counts)
    own, far, rest, mask, pair_v, base_v, flow, values, place, hot, wanted = kept(made)
    extra = pl.pallas_call(
        spare_kernel,
        out_shape=pltpu.VMEM((padded, BLOCK), F32),
        in_specs=[vmem_spec] * 5 + [smem_spec],
        out_specs=vmem_spec,
        scratch_shapes=[pltpu.VMEM((LOT, 2 * capacity), BF16)],
        compiler_params=params(24),
    )(own, rest, mask, values, place, total)
    made = pl.pallas_call(
        functools.partial(main_kernel, n_mon, n_sub, chunk),
        out_shape=[
            pltpu.VMEM((chunks, half, 2 * chunk), F32),
            pltpu.VMEM((chunks, blocks, 2 * chunk), F32),
            pltpu.VMEM((3, capacity), F32),
            pltpu.VMEM((half, BLOCK), F32),
        ],
        in_specs=[vmem_spec] * 11 + [smem_spec],
        out_specs=[vmem_spec] * 4,
        scratch_shapes=[
            pltpu.VMEM((padded, BLOCK), BF16),
            pltpu.VMEM((n - 1, padded, BLOCK), BF16),
            pltpu.VMEM((n_mon - 1, padded, BLOCK), F32),
            pltpu.VMEM((half + tail, width), BF16),
            pltpu.VMEM((n_sub * blocks, width), BF16),
            dma, dma, dma, dma, dma((2,)), dma((2,)),
        ],
        compiler_params=params(40, collective_id=1, has_side_effects=True),
    )(own, far, rest, mask, pair_v, base_v, flow, hot, wanted, place, kept([extra])[0], pair_counts)
    return pl.pallas_call(
        last_kernel,
        out_shape=jax.ShapeDtypeStruct((half, capacity), BF16),
        in_specs=[vmem_spec] * 4,
        out_specs=any_spec,
        scratch_shapes=[pltpu.VMEM((half, capacity), BF16), dma((blocks,))],
        compiler_params=params(16),
    )(*kept(made))


def solution(mesh):
    return jax.shard_map(
        functools.partial(on_device, mesh.shape["mon"], mesh.shape["sub"]),
        mesh=mesh,
        in_specs=(
            P("mon", "sub"),
            P("mon", "sub"),
            P("mon"),
            P(),
            P(("grp", "pair"), None),
            P(("grp", "pair")),
        ),
        out_specs=P(("mon", "sub"), ("grp", "pair")),
        check_vma=False,
    )
```

```python
import functools

import jax
import jax.numpy as jnp
from jax import lax
from jax.experimental import pallas as pl
from jax.experimental.pallas import tpu as pltpu
from jax.sharding import PartitionSpec as P

BLOCK = 128
LOT = 256
MESH = pl.DeviceIdType.MESH
F32 = jnp.float32
BF16 = jnp.bfloat16
I32 = jnp.int32


def lookup(table, index):
    groups = []
    height = table.shape[0]
    for start in range(0, index.shape[1], 128):
        wide = jnp.broadcast_to(index[:, start:start + 128], (height, 128))
        lanes = jnp.take_along_axis(table, wide & 127, axis=1)
        level = lax.broadcasted_iota(I32, (height, 128), 0)
        picked = jnp.where(level == (wide >> 7), lanes, jnp.zeros_like(lanes))
        groups.append(jnp.sum(picked, axis=0, keepdims=True))
    return jnp.concatenate(groups, axis=1)


def stack_groups(wide, height):
    rows = [wide[:, start:start + BLOCK] for start in range(0, wide.shape[1], BLOCK)]
    rows += [jnp.zeros((1, BLOCK), wide.dtype)] * (height - len(rows))
    return jnp.concatenate(rows, axis=0)


def ones_where(condition):
    return jnp.where(condition, F32(1), F32(0)).astype(BF16)


def spread_lot(place_ref, lot, groups, spread_ref):
    level = lax.broadcasted_iota(I32, (LOT, BLOCK), 0) + lot * LOT
    for g in range(groups):
        spread_ref[:, g * BLOCK:(g + 1) * BLOCK] = ones_where(level == place_ref[g:g + 1, :])


def wanted_of(values, spread):
    picked = lax.dot_general(values, spread, (((1,), (1,)), ((), ())), preferred_element_type=F32).astype(I32)
    filled = picked[4:5] > 0
    row = jnp.where(filled, picked[0:1] * 256 + picked[1:2], -1)
    column = jnp.where(filled, picked[2:3] * 256 + picked[3:4], -1)
    return row, column


def found_of(parts, mask, hot, row):
    found = jnp.zeros((1, LOT), F32)
    start = 0
    for part in parts:
        near = jnp.dot(part, hot, preferred_element_type=F32)
        level = lax.broadcasted_iota(I32, near.shape, 0) + start
        found = found + jnp.sum(jnp.where(level == row, near, F32(0)), axis=0, keepdims=True)
        start += part.shape[0]
    kept = jnp.dot(mask, hot, preferred_element_type=F32)
    level = lax.broadcasted_iota(I32, kept.shape, 0)
    return found * jnp.sum(jnp.where(level == (row >> 7), kept, F32(0)), axis=0, keepdims=True)


def scatter(found, place):
    lanes, level = place & (BLOCK - 1), place >> 7
    value = jnp.zeros(place.shape, F32)
    for t in range(LOT // BLOCK):
        wide = jnp.broadcast_to(found[:, t * BLOCK:(t + 1) * BLOCK], place.shape)
        value = value + jnp.where(level == t, jnp.take_along_axis(wide, lanes, axis=1), F32(0))
    return value


def padded_rows(rows):
    pad = jnp.zeros((-rows.shape[0] % 16, rows.shape[1]), F32)
    return jnp.concatenate([rows, pad], axis=0).astype(BF16)


def head_kernel(n_sub, df_hbm, mask_hbm, base_hbm, row_hbm, pair_hbm, count_s,
                own, far, rest, mask, pair_v, base_v, flow, values, place, hot, wanted, total_s,
                row_v, spread, mask_v, far_mask, load_sem, part_send, part_recv):
    rows_dev, width = df_hbm.shape
    half = rows_dev // n_sub
    blocks = half // BLOCK
    capacity = pair_hbm.shape[1]
    groups = 2 * capacity // BLOCK
    mon = lax.axis_index("mon")
    sub = lax.axis_index("sub")
    other = 1 - sub
    partner = {"sub": other}

    barrier = pltpu.get_barrier_semaphore()

    @pl.when(mon == 0)
    def _():
        pl.semaphore_signal(barrier, inc=1, device_id=partner, device_id_type=MESH)

    loads = [
        pltpu.make_async_copy(row_hbm, row_v, load_sem.at[0]),
        pltpu.make_async_copy(pair_hbm, pair_v, load_sem.at[1]),
        pltpu.make_async_copy(df_hbm.at[pl.ds(sub * half, half)], own.at[pl.ds(0, half)], load_sem.at[2]),
        pltpu.make_async_copy(df_hbm.at[pl.ds(other * half, half)], rest, load_sem.at[3]),
        pltpu.make_async_copy(mask_hbm, mask_v, load_sem.at[4]),
        pltpu.make_async_copy(base_hbm, base_v, load_sem.at[5]),
    ]
    for load in loads:
        load.start()
    part_copies = [
        pltpu.make_async_remote_copy(
            df_hbm.at[pl.ds(other * half, half)], far.at[pl.ds(0, half)],
            part_send.at[0], part_recv.at[0], device_id=partner, device_id_type=MESH),
        pltpu.make_async_remote_copy(
            mask_hbm.at[pl.ds(other * blocks, blocks)], far_mask,
            part_send.at[1], part_recv.at[1], device_id=partner, device_id_type=MESH),
    ]

    @pl.when(mon == 0)
    def _():
        pl.semaphore_wait(barrier, 1)
        for copy in part_copies:
            copy.start()

    loads[0].wait()
    loads[1].wait()
    table = row_v[...]
    first, second = pair_v[0:1, :], pair_v[1:2, :]
    first_row, second_row = lookup(table, first), lookup(table, second)
    row = jnp.concatenate([first_row, second_row], axis=1) - mon * rows_dev
    column = jnp.concatenate([second, first], axis=1) - sub * width
    slot = lax.broadcasted_iota(I32, (1, capacity), 1)
    live = slot < count_s[0]
    live = jnp.concatenate([live, live], axis=1)
    local = (row >= 0) & (row < rows_dev) & (column >= 0) & (column < width) & live
    flags = jnp.where(local, F32(1), F32(0))
    running = jnp.zeros((1, BLOCK), F32)
    flag_rows, before_rows = [], []
    for g in range(groups):
        flag_rows.append(flags[:, g * BLOCK:(g + 1) * BLOCK])
        before_rows.append(running)
        running = running + flag_rows[-1]
    padding = [jnp.zeros((1, BLOCK), F32)] * (place.shape[0] - groups)
    flag_grid = jnp.concatenate(flag_rows + padding, axis=0)
    counted = jnp.concatenate([flag_grid, jnp.concatenate(before_rows + padding, axis=0)], axis=1)
    across = lax.broadcasted_iota(I32, (2 * BLOCK, BLOCK), 0)
    down = lax.broadcasted_iota(I32, (2 * BLOCK, BLOCK), 1)
    adder = ones_where((across < down) | (across >= BLOCK))
    order = jnp.dot(counted.astype(BF16), adder, preferred_element_type=F32).astype(I32)
    place[...] = jnp.where(flag_grid > 0, order, -1)
    zero = jnp.zeros_like(row)
    stacked = jnp.concatenate([row >> 8, row & 255, column >> 8, column & 255, zero + 1, zero, zero, zero], axis=0)
    values[...] = stacked.astype(F32).astype(BF16)
    spread_lot(place, 0, groups, spread)
    wanted_row, wanted_column = wanted_of(values[...], spread[...])
    wanted[...] = wanted_row
    level = lax.broadcasted_iota(I32, (width, LOT), 0)
    hot[...] = ones_where(level == wanted_column)
    total_s[0] = jnp.sum(running).astype(I32)

    loads[5].wait()
    base = base_v[...]
    flow[...] = stack_groups(lookup(base, row), flow.shape[0])
    loads[4].wait()
    whole = mask_v[...].astype(F32)
    low, high = whole[:blocks], whole[blocks:]
    swapped = sub != 0
    mine, theirs = jnp.where(swapped, high, low), jnp.where(swapped, low, high)
    mask[...] = jnp.concatenate([mine, theirs], axis=0).astype(BF16)
    for load in loads[2:4]:
        load.wait()
    own[half:, :] = padded_rows(mine)

    @pl.when(mon == 0)
    def _():
        for copy in part_copies:
            copy.wait_recv()
        far[half:, :] = padded_rows(far_mask[...].astype(F32))
        for copy in part_copies:
            copy.wait_send()


def order_rows(row, half, sub):
    flipped = jnp.where(row >= half, row - half, row + half)
    return jnp.where(row < 0, -1, jnp.where(sub == 0, row, flipped))


def spare_kernel(own, rest, mask, values, place, total_s, extra, spread):
    half, width = rest.shape
    groups = values.shape[1] // BLOCK
    sub = lax.axis_index("sub")
    extra[...] = jnp.zeros_like(extra)

    def one_lot(lot, carry):
        spread_lot(place, lot, groups, spread)
        row, column = wanted_of(values[...], spread[...])
        row = order_rows(row, half, sub)
        level = lax.broadcasted_iota(I32, (width, LOT), 0)
        hot = ones_where(level == column)
        found = found_of([own[0:half, :], rest[...]], mask[...], hot, row)
        extra[...] += scatter(found, place[...] - lot * LOT)
        return carry

    lax.fori_loop(1, (total_s[0] + LOT - 1) // LOT, one_lot, 0)


def main_kernel(n_mon, n_sub, chunk, own, first_far, rest, mask, pair_v, base_v, flow, hot, wanted, place, extra, count_s,
                product, keep, shifts, base_wide,
                told, cross_got, flow_got, far, far_mask, cross_send, cross_recv, flow_send, flow_recv, part_send, part_recv):
    half, width = rest.shape
    blocks = half // BLOCK
    capacity = pair_v.shape[1]
    chunks = capacity // chunk
    n = n_mon * n_sub
    mon = lax.axis_index("mon")
    sub = lax.axis_index("sub")
    other = 1 - sub
    me = mon * n_sub + sub

    def peer(step):
        flat = lax.rem(me + step, n)
        return {"mon": flat // n_sub, "sub": lax.rem(flat, n_sub)}

    barrier = pltpu.get_barrier_semaphore()

    def greet(step, carry):
        pl.semaphore_signal(barrier, inc=1, device_id=peer(step), device_id_type=MESH)
        return carry

    lax.fori_loop(1, n, greet, 0)
    row = order_rows(wanted[...], half, sub)
    found = found_of([own[0:half, :], rest[...]], mask[...], hot[...], row)

    def tell():
        told[...] = (scatter(found, place[...]) + extra[...]).astype(BF16)

    late = mon > n_mon // 2

    @pl.when(jnp.logical_not(late))
    def _():
        tell()

    def hot_columns(c, side):
        span = pl.ds(c * chunk if isinstance(c, int) else pl.multiple_of(c * chunk, chunk), chunk)
        columns = jnp.concatenate([pair_v[0:1, span], pair_v[1:2, span]], axis=1) - side * width
        level = lax.broadcasted_iota(I32, (width, 2 * chunk), 0)
        return ones_where(level == columns)

    def make(far_ref):
        def one_chunk(c, carry):
            whole = jnp.concatenate([own[...], far_ref[...]], axis=1)
            columns = jnp.concatenate([hot_columns(c, sub), hot_columns(c, other)], axis=0)
            made = jnp.dot(whole, columns, preferred_element_type=F32)
            product[c] = made[:half].astype(product.dtype)
            keep[c] = made[half:half + blocks]
            return carry

        return one_chunk

    def near_chunk(c, carry):
        made = jnp.dot(own[...], hot_columns(c, sub), preferred_element_type=F32)
        product[c] = made[:half].astype(product.dtype)
        keep[c] = made[half:half + blocks]
        return carry

    def far_chunk(c, carry):
        made = jnp.dot(far[...], hot_columns(c, other), preferred_element_type=F32)
        product[c] = (product[c].astype(F32) + made[:half]).astype(product.dtype)
        keep[c] += made[half:half + blocks]
        return carry

    early = mon < n_mon // 2
    root = (lax.axis_index("grp") == 0) & (lax.axis_index("pair") == 0)
    ahead = jnp.where(root, chunks - 1, 1)

    @pl.when(mon == 0)
    def _():
        lax.fori_loop(0, ahead, make(first_far), 0)

    @pl.when((mon != 0) & early)
    def _():
        for c in range(chunks):
            near_chunk(c, 0)

    pl.semaphore_wait(barrier, n - 1)

    def send_flow(i, carry):
        to = i + (i >= mon).astype(I32)
        pltpu.make_async_remote_copy(
            flow, flow_got.at[lax.rem(to + n_mon - mon, n_mon) - 1], flow_send, flow_recv,
            device_id={"mon": to}, device_id_type=MESH).start()
        return carry

    def send(i, carry):
        to = i + (i >= me).astype(I32)
        pltpu.make_async_remote_copy(
            told, cross_got.at[lax.rem(to + n - me, n) - 1], cross_send, cross_recv,
            device_id={"mon": to // n_sub, "sub": lax.rem(to, n_sub)}, device_id_type=MESH).start()
        return carry

    lax.fori_loop(0, n_mon - 1, send_flow, 0)

    @pl.when(late)
    def _():
        tell()

    lax.fori_loop(0, n - 1, send, 0)
    partner = {"sub": other}
    part_copies = [
        pltpu.make_async_remote_copy(
            rest, far.at[pl.ds(0, half)],
            part_send.at[0], part_recv.at[0], device_id=partner, device_id_type=MESH),
        pltpu.make_async_remote_copy(
            mask, far_mask,
            part_send.at[1], part_recv.at[1], device_id=partner, device_id_type=MESH),
    ]

    @pl.when(mon != 0)
    def _():
        for copy in part_copies:
            copy.start()

    base = jnp.where(sub == 0, base_v[0:blocks], base_v[blocks:2 * blocks])
    for b in range(blocks):
        base_wide[b * BLOCK:(b + 1) * BLOCK, :] = jnp.broadcast_to(base[b:b + 1, :], (BLOCK, BLOCK)).T

    @pl.when(mon == 0)
    def _():
        lax.fori_loop(ahead, chunks, make(first_far), 0)

    @pl.when(jnp.logical_not(early))
    def _():
        for c in range(chunks):
            near_chunk(c, 0)

    @pl.when(mon != 0)
    def _():
        for copy in part_copies:
            copy.wait_recv()
        far[half:, :] = padded_rows(far_mask[...].astype(F32)[blocks:])
        for c in range(chunks):
            far_chunk(c, 0)
        for copy in part_copies:
            copy.wait_send()

    live = (lax.broadcasted_iota(I32, (1, capacity), 1) < count_s[0]).astype(F32)
    pltpu.make_async_copy(flow_got, flow_got, flow_recv).wait()
    flows = flow[...] + jnp.sum(flow_got[...], axis=0)
    pltpu.make_async_copy(cross_got, cross_got, cross_recv).wait()
    cross = told[...].astype(F32) + jnp.sum(cross_got[...].astype(F32), axis=0)
    rows = capacity // BLOCK
    cross_first, cross_second = cross[:rows], cross[rows:2 * rows]
    flow_first, flow_second = flows[:rows], flows[rows:2 * rows]
    determinant = 1.0 - cross_first * cross_second
    shift_first = ((flow_first + cross_first * flow_second) / determinant).astype(BF16).astype(F32)
    shift_second = ((flow_second + cross_second * flow_first) / determinant).astype(BF16).astype(F32)
    for g in range(rows):
        span = slice(g * BLOCK, (g + 1) * BLOCK)
        shifts[0:1, span] = shift_first[g:g + 1] * live[:, span]
        shifts[1:2, span] = shift_second[g:g + 1] * live[:, span]
    shifts[2:3, :] = live
    pltpu.make_async_copy(flow_got, flow_got, flow_send).wait()
    pltpu.make_async_copy(cross_got, cross_got, cross_send).wait()


def last_kernel(product, keep, shifts, base_wide, out_hbm, out_v, sems):
    chunks, half, pair_width = product.shape
    chunk = pair_width // 2
    copies = []
    for b in range(half // BLOCK):
        rows = slice(b * BLOCK, (b + 1) * BLOCK)
        flows = jnp.concatenate([base_wide[rows, :]] * (chunk // BLOCK), axis=1)
        for c in range(chunks):
            span = slice(c * chunk, (c + 1) * chunk)
            effect_first = shifts[0:1, span] * keep[c, b:b + 1, :chunk]
            effect_second = shifts[1:2, span] * keep[c, b:b + 1, chunk:]
            value = flows * shifts[2:3, span] + product[c, rows, :chunk] * effect_first
            value = value + product[c, rows, chunk:] * effect_second
            out_v[rows, span] = value.astype(BF16)
        place = pl.ds(b * BLOCK, BLOCK)
        copies.append(pltpu.make_async_copy(out_v.at[place], out_hbm.at[place], sems.at[b]))
        copies[-1].start()
    for copy in copies:
        copy.wait()


def on_device(n_mon, n_sub, dfactors, block_mask, base_flow, branch_row, pair_slots, pair_counts):
    rows_dev, width = dfactors.shape
    half = rows_dev // n_sub
    blocks = half // BLOCK
    tail = -(-blocks // 16) * 16
    capacity = pair_slots.shape[0]
    chunk = 256 if capacity % 256 == 0 else BLOCK
    chunks = capacity // chunk
    groups = 2 * capacity // BLOCK
    padded = -(-groups // 16) * 16
    n = n_mon * n_sub
    any_spec = pl.BlockSpec(memory_space=pltpu.HBM)
    vmem_spec = pl.BlockSpec(memory_space=pltpu.VMEM)
    smem_spec = pl.BlockSpec(memory_space=pltpu.SMEM)
    dma = pltpu.SemaphoreType.DMA

    def params(mib, **more):
        return pltpu.CompilerParams(vmem_limit_bytes=int(mib * 1024 * 1024), **more)

    def kept(arrays):
        return [pltpu.with_memory_space_constraint(array, pltpu.VMEM) for array in arrays]

    *made, total = pl.pallas_call(
        functools.partial(head_kernel, n_sub),
        out_shape=[
            pltpu.VMEM((half + tail, width), BF16),
            pltpu.VMEM((half + tail, width), BF16),
            pltpu.VMEM((half, width), BF16),
            pltpu.VMEM((n_sub * blocks, width), BF16),
            pltpu.VMEM((2, capacity), I32),
            pltpu.VMEM((n_sub * blocks, BLOCK), F32),
            pltpu.VMEM((padded, BLOCK), F32),
            pltpu.VMEM((8, 2 * capacity), BF16),
            pltpu.VMEM((padded, BLOCK), I32),
            pltpu.VMEM((width, LOT), BF16),
            pltpu.VMEM((1, LOT), I32),
            pltpu.SMEM((1,), I32),
        ],
        in_specs=[any_spec] * 5 + [smem_spec],
        out_specs=[vmem_spec] * 11 + [smem_spec],
        scratch_shapes=[
            pltpu.VMEM((branch_row.shape[0] // BLOCK, BLOCK), I32),
            pltpu.VMEM((LOT, 2 * capacity), BF16),
            pltpu.VMEM((n_sub * blocks, width), I32),
            pltpu.VMEM((blocks, width), I32),
            dma((6,)), dma((2,)), dma((2,)),
        ],
        compiler_params=params(58.8, collective_id=0, has_side_effects=True),
    )(dfactors, block_mask, base_flow.reshape(-1, BLOCK), branch_row.reshape(-1, BLOCK), pair_slots.T, pair_counts)
    own, far, rest, mask, pair_v, base_v, flow, values, place, hot, wanted = kept(made)
    extra = pl.pallas_call(
        spare_kernel,
        out_shape=pltpu.VMEM((padded, BLOCK), F32),
        in_specs=[vmem_spec] * 5 + [smem_spec],
        out_specs=vmem_spec,
        scratch_shapes=[pltpu.VMEM((LOT, 2 * capacity), BF16)],
        compiler_params=params(24),
    )(own, rest, mask, values, place, total)
    made = pl.pallas_call(
        functools.partial(main_kernel, n_mon, n_sub, chunk),
        out_shape=[
            pltpu.VMEM((chunks, half, 2 * chunk), F32),
            pltpu.VMEM((chunks, blocks, 2 * chunk), F32),
            pltpu.VMEM((3, capacity), F32),
            pltpu.VMEM((half, BLOCK), F32),
        ],
        in_specs=[vmem_spec] * 11 + [smem_spec],
        out_specs=[vmem_spec] * 4,
        scratch_shapes=[
            pltpu.VMEM((padded, BLOCK), BF16),
            pltpu.VMEM((n - 1, padded, BLOCK), BF16),
            pltpu.VMEM((n_mon - 1, padded, BLOCK), F32),
            pltpu.VMEM((half + tail, width), BF16),
            pltpu.VMEM((n_sub * blocks, width), BF16),
            dma, dma, dma, dma, dma((2,)), dma((2,)),
        ],
        compiler_params=params(40, collective_id=1, has_side_effects=True),
    )(own, far, rest, mask, pair_v, base_v, flow, hot, wanted, place, kept([extra])[0], pair_counts)
    return pl.pallas_call(
        last_kernel,
        out_shape=jax.ShapeDtypeStruct((half, capacity), BF16),
        in_specs=[vmem_spec] * 4,
        out_specs=any_spec,
        scratch_shapes=[pltpu.VMEM((half, capacity), BF16), dma((blocks,))],
        compiler_params=params(16),
    )(*kept(made))


def solution(mesh):
    return jax.shard_map(
        functools.partial(on_device, mesh.shape["mon"], mesh.shape["sub"]),
        mesh=mesh,
        in_specs=(
            P("mon", "sub"),
            P("mon", "sub"),
            P("mon"),
            P(),
            P(("grp", "pair"), None),
            P(("grp", "pair")),
        ),
        out_specs=P(("mon", "sub"), ("grp", "pair")),
        check_vma=False,
    )
```

```python
import functools

import jax
import jax.numpy as jnp
from jax import lax
from jax.experimental import pallas as pl
from jax.experimental.pallas import tpu as pltpu
from jax.sharding import PartitionSpec as P

BLOCK = 128
LOT = 256
MESH = pl.DeviceIdType.MESH
F32 = jnp.float32
BF16 = jnp.bfloat16
I32 = jnp.int32


def lookup(table, index):
    groups = []
    height = table.shape[0]
    for start in range(0, index.shape[1], 128):
        wide = jnp.broadcast_to(index[:, start:start + 128], (height, 128))
        lanes = jnp.take_along_axis(table, wide & 127, axis=1)
        level = lax.broadcasted_iota(I32, (height, 128), 0)
        picked = jnp.where(level == (wide >> 7), lanes, jnp.zeros_like(lanes))
        groups.append(jnp.sum(picked, axis=0, keepdims=True))
    return jnp.concatenate(groups, axis=1)


def stack_groups(wide, height):
    rows = [wide[:, start:start + BLOCK] for start in range(0, wide.shape[1], BLOCK)]
    rows += [jnp.zeros((1, BLOCK), wide.dtype)] * (height - len(rows))
    return jnp.concatenate(rows, axis=0)


def ones_where(condition):
    return jnp.where(condition, F32(1), F32(0)).astype(BF16)


def spread_lot(place_ref, lot, groups, spread_ref):
    level = lax.broadcasted_iota(I32, (LOT, BLOCK), 0) + lot * LOT
    for g in range(groups):
        spread_ref[:, g * BLOCK:(g + 1) * BLOCK] = ones_where(level == place_ref[g:g + 1, :])


def wanted_of(values, spread):
    picked = lax.dot_general(values, spread, (((1,), (1,)), ((), ())), preferred_element_type=F32).astype(I32)
    filled = picked[4:5] > 0
    row = jnp.where(filled, picked[0:1] * 256 + picked[1:2], -1)
    column = jnp.where(filled, picked[2:3] * 256 + picked[3:4], -1)
    return row, column


def found_of(parts, mask, hot, row):
    found = jnp.zeros((1, LOT), F32)
    start = 0
    for part in parts:
        near = jnp.dot(part, hot, preferred_element_type=F32)
        level = lax.broadcasted_iota(I32, near.shape, 0) + start
        found = found + jnp.sum(jnp.where(level == row, near, F32(0)), axis=0, keepdims=True)
        start += part.shape[0]
    kept = jnp.dot(mask, hot, preferred_element_type=F32)
    level = lax.broadcasted_iota(I32, kept.shape, 0)
    return found * jnp.sum(jnp.where(level == (row >> 7), kept, F32(0)), axis=0, keepdims=True)


def scatter(found, place):
    lanes, level = place & (BLOCK - 1), place >> 7
    value = jnp.zeros(place.shape, F32)
    for t in range(LOT // BLOCK):
        wide = jnp.broadcast_to(found[:, t * BLOCK:(t + 1) * BLOCK], place.shape)
        value = value + jnp.where(level == t, jnp.take_along_axis(wide, lanes, axis=1), F32(0))
    return value


def padded_rows(rows):
    pad = jnp.zeros((-rows.shape[0] % 16, rows.shape[1]), F32)
    return jnp.concatenate([rows, pad], axis=0).astype(BF16)


def head_kernel(n_sub, df_hbm, mask_hbm, base_hbm, row_hbm, pair_hbm, count_s,
                own, far, rest, mask, pair_v, base_v, flow, values, place, hot, wanted, total_s,
                row_v, spread, mask_v, far_mask, load_sem, part_send, part_recv):
    rows_dev, width = df_hbm.shape
    half = rows_dev // n_sub
    blocks = half // BLOCK
    capacity = pair_hbm.shape[1]
    groups = 2 * capacity // BLOCK
    mon = lax.axis_index("mon")
    sub = lax.axis_index("sub")
    other = 1 - sub
    partner = {"sub": other}

    barrier = pltpu.get_barrier_semaphore()

    @pl.when(mon == 0)
    def _():
        pl.semaphore_signal(barrier, inc=1, device_id=partner, device_id_type=MESH)

    loads = [
        pltpu.make_async_copy(row_hbm, row_v, load_sem.at[0]),
        pltpu.make_async_copy(pair_hbm, pair_v, load_sem.at[1]),
        pltpu.make_async_copy(df_hbm.at[pl.ds(sub * half, half)], own.at[pl.ds(0, half)], load_sem.at[2]),
        pltpu.make_async_copy(df_hbm.at[pl.ds(other * half, half)], rest, load_sem.at[3]),
        pltpu.make_async_copy(mask_hbm, mask_v, load_sem.at[4]),
        pltpu.make_async_copy(base_hbm, base_v, load_sem.at[5]),
    ]
    for load in loads:
        load.start()
    part_copies = [
        pltpu.make_async_remote_copy(
            df_hbm.at[pl.ds(other * half, half)], far.at[pl.ds(0, half)],
            part_send.at[0], part_recv.at[0], device_id=partner, device_id_type=MESH),
        pltpu.make_async_remote_copy(
            mask_hbm.at[pl.ds(other * blocks, blocks)], far_mask,
            part_send.at[1], part_recv.at[1], device_id=partner, device_id_type=MESH),
    ]

    @pl.when(mon == 0)
    def _():
        pl.semaphore_wait(barrier, 1)
        for copy in part_copies:
            copy.start()

    loads[0].wait()
    loads[1].wait()
    table = row_v[...]
    first, second = pair_v[0:1, :], pair_v[1:2, :]
    first_row, second_row = lookup(table, first), lookup(table, second)
    row = jnp.concatenate([first_row, second_row], axis=1) - mon * rows_dev
    column = jnp.concatenate([second, first], axis=1) - sub * width
    slot = lax.broadcasted_iota(I32, (1, capacity), 1)
    live = slot < count_s[0]
    live = jnp.concatenate([live, live], axis=1)
    local = (row >= 0) & (row < rows_dev) & (column >= 0) & (column < width) & live
    flags = jnp.where(local, F32(1), F32(0))
    running = jnp.zeros((1, BLOCK), F32)
    flag_rows, before_rows = [], []
    for g in range(groups):
        flag_rows.append(flags[:, g * BLOCK:(g + 1) * BLOCK])
        before_rows.append(running)
        running = running + flag_rows[-1]
    padding = [jnp.zeros((1, BLOCK), F32)] * (place.shape[0] - groups)
    flag_grid = jnp.concatenate(flag_rows + padding, axis=0)
    counted = jnp.concatenate([flag_grid, jnp.concatenate(before_rows + padding, axis=0)], axis=1)
    across = lax.broadcasted_iota(I32, (2 * BLOCK, BLOCK), 0)
    down = lax.broadcasted_iota(I32, (2 * BLOCK, BLOCK), 1)
    adder = ones_where((across < down) | (across >= BLOCK))
    order = jnp.dot(counted.astype(BF16), adder, preferred_element_type=F32).astype(I32)
    place[...] = jnp.where(flag_grid > 0, order, -1)
    zero = jnp.zeros_like(row)
    stacked = jnp.concatenate([row >> 8, row & 255, column >> 8, column & 255, zero + 1, zero, zero, zero], axis=0)
    values[...] = stacked.astype(F32).astype(BF16)
    spread_lot(place, 0, groups, spread)
    wanted_row, wanted_column = wanted_of(values[...], spread[...])
    wanted[...] = wanted_row
    level = lax.broadcasted_iota(I32, (width, LOT), 0)
    hot[...] = ones_where(level == wanted_column)
    total_s[0] = jnp.sum(running).astype(I32)

    loads[5].wait()
    base = base_v[...]
    flow[...] = stack_groups(lookup(base, row), flow.shape[0])
    loads[4].wait()
    whole = mask_v[...].astype(F32)
    low, high = whole[:blocks], whole[blocks:]
    swapped = sub != 0
    mine, theirs = jnp.where(swapped, high, low), jnp.where(swapped, low, high)
    mask[...] = jnp.concatenate([mine, theirs], axis=0).astype(BF16)
    for load in loads[2:4]:
        load.wait()
    own[half:, :] = padded_rows(mine)

    @pl.when(mon == 0)
    def _():
        for copy in part_copies:
            copy.wait_recv()
        far[half:, :] = padded_rows(far_mask[...].astype(F32))
        for copy in part_copies:
            copy.wait_send()


def order_rows(row, half, sub):
    flipped = jnp.where(row >= half, row - half, row + half)
    return jnp.where(row < 0, -1, jnp.where(sub == 0, row, flipped))


def spare_kernel(own, rest, mask, values, place, total_s, extra, spread):
    half, width = rest.shape
    groups = values.shape[1] // BLOCK
    sub = lax.axis_index("sub")
    extra[...] = jnp.zeros_like(extra)

    def one_lot(lot, carry):
        spread_lot(place, lot, groups, spread)
        row, column = wanted_of(values[...], spread[...])
        row = order_rows(row, half, sub)
        level = lax.broadcasted_iota(I32, (width, LOT), 0)
        hot = ones_where(level == column)
        found = found_of([own[0:half, :], rest[...]], mask[...], hot, row)
        extra[...] += scatter(found, place[...] - lot * LOT)
        return carry

    lax.fori_loop(1, (total_s[0] + LOT - 1) // LOT, one_lot, 0)


def main_kernel(n_mon, n_sub, chunk, own, first_far, rest, mask, pair_v, base_v, flow, hot, wanted, place, extra, count_s,
                product, keep, shifts, base_wide,
                told, cross_got, flow_got, far, far_mask, cross_send, cross_recv, flow_send, flow_recv, part_send, part_recv):
    half, width = rest.shape
    blocks = half // BLOCK
    capacity = pair_v.shape[1]
    chunks = capacity // chunk
    n = n_mon * n_sub
    mon = lax.axis_index("mon")
    sub = lax.axis_index("sub")
    other = 1 - sub
    me = mon * n_sub + sub

    def peer(step):
        flat = lax.rem(me + step, n)
        return {"mon": flat // n_sub, "sub": lax.rem(flat, n_sub)}

    barrier = pltpu.get_barrier_semaphore()

    def greet(step, carry):
        pl.semaphore_signal(barrier, inc=1, device_id=peer(step), device_id_type=MESH)
        return carry

    lax.fori_loop(1, n, greet, 0)
    row = order_rows(wanted[...], half, sub)
    found = found_of([own[0:half, :], rest[...]], mask[...], hot[...], row)

    def tell():
        told[...] = (scatter(found, place[...]) + extra[...]).astype(BF16)

    late = mon > n_mon // 2

    @pl.when(jnp.logical_not(late))
    def _():
        tell()

    def hot_columns(c, side):
        span = pl.ds(c * chunk if isinstance(c, int) else pl.multiple_of(c * chunk, chunk), chunk)
        columns = jnp.concatenate([pair_v[0:1, span], pair_v[1:2, span]], axis=1) - side * width
        level = lax.broadcasted_iota(I32, (width, 2 * chunk), 0)
        return ones_where(level == columns)

    def make(far_ref):
        def one_chunk(c, carry):
            whole = jnp.concatenate([own[...], far_ref[...]], axis=1)
            columns = jnp.concatenate([hot_columns(c, sub), hot_columns(c, other)], axis=0)
            made = jnp.dot(whole, columns, preferred_element_type=F32)
            product[c] = made[:half].astype(product.dtype)
            keep[c] = made[half:half + blocks]
            return carry

        return one_chunk

    def near_chunk(c, carry):
        made = jnp.dot(own[...], hot_columns(c, sub), preferred_element_type=F32)
        product[c] = made[:half].astype(product.dtype)
        keep[c] = made[half:half + blocks]
        return carry

    def far_chunk(c, carry):
        made = jnp.dot(far[...], hot_columns(c, other), preferred_element_type=F32)
        product[c] = (product[c].astype(F32) + made[:half]).astype(product.dtype)
        keep[c] += made[half:half + blocks]
        return carry

    early = mon < n_mon // 2
    root = (lax.axis_index("grp") == 0) & (lax.axis_index("pair") == 0)
    ahead = jnp.where(root, chunks - 1, 1)

    @pl.when(mon == 0)
    def _():
        lax.fori_loop(0, ahead, make(first_far), 0)

    @pl.when((mon != 0) & early)
    def _():
        for c in range(chunks):
            near_chunk(c, 0)

    pl.semaphore_wait(barrier, n - 1)

    def send_flow(i, carry):
        to = i + (i >= mon).astype(I32)
        pltpu.make_async_remote_copy(
            flow, flow_got.at[lax.rem(to + n_mon - mon, n_mon) - 1], flow_send, flow_recv,
            device_id={"mon": to}, device_id_type=MESH).start()
        return carry

    def send(i, carry):
        to = i + (i >= me).astype(I32)
        pltpu.make_async_remote_copy(
            told, cross_got.at[lax.rem(to + n - me, n) - 1], cross_send, cross_recv,
            device_id={"mon": to // n_sub, "sub": lax.rem(to, n_sub)}, device_id_type=MESH).start()
        return carry

    partner = {"sub": other}
    part_copies = [
        pltpu.make_async_remote_copy(
            rest, far.at[pl.ds(0, half)],
            part_send.at[0], part_recv.at[0], device_id=partner, device_id_type=MESH),
        pltpu.make_async_remote_copy(
            mask, far_mask,
            part_send.at[1], part_recv.at[1], device_id=partner, device_id_type=MESH),
    ]

    @pl.when((mon != 0) & early)
    def _():
        for copy in part_copies:
            copy.start()

    lax.fori_loop(0, n_mon - 1, send_flow, 0)

    @pl.when(late)
    def _():
        tell()

    lax.fori_loop(0, n - 1, send, 0)

    @pl.when(jnp.logical_not(early))
    def _():
        for copy in part_copies:
            copy.start()

    base = jnp.where(sub == 0, base_v[0:blocks], base_v[blocks:2 * blocks])
    for b in range(blocks):
        base_wide[b * BLOCK:(b + 1) * BLOCK, :] = jnp.broadcast_to(base[b:b + 1, :], (BLOCK, BLOCK)).T

    @pl.when(mon == 0)
    def _():
        lax.fori_loop(ahead, chunks, make(first_far), 0)

    @pl.when(jnp.logical_not(early))
    def _():
        for c in range(chunks):
            near_chunk(c, 0)

    @pl.when(mon != 0)
    def _():
        for copy in part_copies:
            copy.wait_recv()
        far[half:, :] = padded_rows(far_mask[...].astype(F32)[blocks:])
        for c in range(chunks):
            far_chunk(c, 0)
        for copy in part_copies:
            copy.wait_send()

    live = (lax.broadcasted_iota(I32, (1, capacity), 1) < count_s[0]).astype(F32)
    pltpu.make_async_copy(flow_got, flow_got, flow_recv).wait()
    flows = flow[...] + jnp.sum(flow_got[...], axis=0)
    pltpu.make_async_copy(cross_got, cross_got, cross_recv).wait()
    cross = told[...].astype(F32) + jnp.sum(cross_got[...].astype(F32), axis=0)
    rows = capacity // BLOCK
    cross_first, cross_second = cross[:rows], cross[rows:2 * rows]
    flow_first, flow_second = flows[:rows], flows[rows:2 * rows]
    determinant = 1.0 - cross_first * cross_second
    shift_first = ((flow_first + cross_first * flow_second) / determinant).astype(BF16).astype(F32)
    shift_second = ((flow_second + cross_second * flow_first) / determinant).astype(BF16).astype(F32)
    for g in range(rows):
        span = slice(g * BLOCK, (g + 1) * BLOCK)
        shifts[0:1, span] = shift_first[g:g + 1] * live[:, span]
        shifts[1:2, span] = shift_second[g:g + 1] * live[:, span]
    shifts[2:3, :] = live
    pltpu.make_async_copy(flow_got, flow_got, flow_send).wait()
    pltpu.make_async_copy(cross_got, cross_got, cross_send).wait()


def last_kernel(product, keep, shifts, base_wide, out_hbm, out_v, sems):
    chunks, half, pair_width = product.shape
    chunk = pair_width // 2
    copies = []
    for b in range(half // BLOCK):
        rows = slice(b * BLOCK, (b + 1) * BLOCK)
        flows = jnp.concatenate([base_wide[rows, :]] * (chunk // BLOCK), axis=1)
        for c in range(chunks):
            span = slice(c * chunk, (c + 1) * chunk)
            effect_first = shifts[0:1, span] * keep[c, b:b + 1, :chunk]
            effect_second = shifts[1:2, span] * keep[c, b:b + 1, chunk:]
            value = flows * shifts[2:3, span] + product[c, rows, :chunk] * effect_first
            value = value + product[c, rows, chunk:] * effect_second
            out_v[rows, span] = value.astype(BF16)
        place = pl.ds(b * BLOCK, BLOCK)
        copies.append(pltpu.make_async_copy(out_v.at[place], out_hbm.at[place], sems.at[b]))
        copies[-1].start()
    for copy in copies:
        copy.wait()


def on_device(n_mon, n_sub, dfactors, block_mask, base_flow, branch_row, pair_slots, pair_counts):
    rows_dev, width = dfactors.shape
    half = rows_dev // n_sub
    blocks = half // BLOCK
    tail = -(-blocks // 16) * 16
    capacity = pair_slots.shape[0]
    chunk = 256 if capacity % 256 == 0 else BLOCK
    chunks = capacity // chunk
    groups = 2 * capacity // BLOCK
    padded = -(-groups // 16) * 16
    n = n_mon * n_sub
    any_spec = pl.BlockSpec(memory_space=pltpu.HBM)
    vmem_spec = pl.BlockSpec(memory_space=pltpu.VMEM)
    smem_spec = pl.BlockSpec(memory_space=pltpu.SMEM)
    dma = pltpu.SemaphoreType.DMA

    def params(mib, **more):
        return pltpu.CompilerParams(vmem_limit_bytes=int(mib * 1024 * 1024), **more)

    def kept(arrays):
        return [pltpu.with_memory_space_constraint(array, pltpu.VMEM) for array in arrays]

    *made, total = pl.pallas_call(
        functools.partial(head_kernel, n_sub),
        out_shape=[
            pltpu.VMEM((half + tail, width), BF16),
            pltpu.VMEM((half + tail, width), BF16),
            pltpu.VMEM((half, width), BF16),
            pltpu.VMEM((n_sub * blocks, width), BF16),
            pltpu.VMEM((2, capacity), I32),
            pltpu.VMEM((n_sub * blocks, BLOCK), F32),
            pltpu.VMEM((padded, BLOCK), F32),
            pltpu.VMEM((8, 2 * capacity), BF16),
            pltpu.VMEM((padded, BLOCK), I32),
            pltpu.VMEM((width, LOT), BF16),
            pltpu.VMEM((1, LOT), I32),
            pltpu.SMEM((1,), I32),
        ],
        in_specs=[any_spec] * 5 + [smem_spec],
        out_specs=[vmem_spec] * 11 + [smem_spec],
        scratch_shapes=[
            pltpu.VMEM((branch_row.shape[0] // BLOCK, BLOCK), I32),
            pltpu.VMEM((LOT, 2 * capacity), BF16),
            pltpu.VMEM((n_sub * blocks, width), I32),
            pltpu.VMEM((blocks, width), I32),
            dma((6,)), dma((2,)), dma((2,)),
        ],
        compiler_params=params(58.8, collective_id=0, has_side_effects=True),
    )(dfactors, block_mask, base_flow.reshape(-1, BLOCK), branch_row.reshape(-1, BLOCK), pair_slots.T, pair_counts)
    own, far, rest, mask, pair_v, base_v, flow, values, place, hot, wanted = kept(made)
    extra = pl.pallas_call(
        spare_kernel,
        out_shape=pltpu.VMEM((padded, BLOCK), F32),
        in_specs=[vmem_spec] * 5 + [smem_spec],
        out_specs=vmem_spec,
        scratch_shapes=[pltpu.VMEM((LOT, 2 * capacity), BF16)],
        compiler_params=params(24),
    )(own, rest, mask, values, place, total)
    made = pl.pallas_call(
        functools.partial(main_kernel, n_mon, n_sub, chunk),
        out_shape=[
            pltpu.VMEM((chunks, half, 2 * chunk), F32),
            pltpu.VMEM((chunks, blocks, 2 * chunk), F32),
            pltpu.VMEM((3, capacity), F32),
            pltpu.VMEM((half, BLOCK), F32),
        ],
        in_specs=[vmem_spec] * 11 + [smem_spec],
        out_specs=[vmem_spec] * 4,
        scratch_shapes=[
            pltpu.VMEM((padded, BLOCK), BF16),
            pltpu.VMEM((n - 1, padded, BLOCK), BF16),
            pltpu.VMEM((n_mon - 1, padded, BLOCK), F32),
            pltpu.VMEM((half + tail, width), BF16),
            pltpu.VMEM((n_sub * blocks, width), BF16),
            dma, dma, dma, dma, dma((2,)), dma((2,)),
        ],
        compiler_params=params(40, collective_id=1, has_side_effects=True),
    )(own, far, rest, mask, pair_v, base_v, flow, hot, wanted, place, kept([extra])[0], pair_counts)
    return pl.pallas_call(
        last_kernel,
        out_shape=jax.ShapeDtypeStruct((half, capacity), BF16),
        in_specs=[vmem_spec] * 4,
        out_specs=any_spec,
        scratch_shapes=[pltpu.VMEM((half, capacity), BF16), dma((blocks,))],
        compiler_params=params(16),
    )(*kept(made))


def solution(mesh):
    return jax.shard_map(
        functools.partial(on_device, mesh.shape["mon"], mesh.shape["sub"]),
        mesh=mesh,
        in_specs=(
            P("mon", "sub"),
            P("mon", "sub"),
            P("mon"),
            P(),
            P(("grp", "pair"), None),
            P(("grp", "pair")),
        ),
        out_specs=P(("mon", "sub"), ("grp", "pair")),
        check_vma=False,
    )
```
